256 devices in a mesh: row: 16 (over z, core), col: 16 (over x, y).
Axes of the slice: x: 4, y: 4, z: 8, core: 2. Of those that a mesh axis runs over, the one named last changes fastest.
Arguments:
- tensor: float32 [12, 8192, 8192], P(None, 'row', 'col'), may hold values from -6 to 6
- factor_b: float32 [8192, 128], P(('col', 'row')), may hold values from -0.0625 to 0.0625
- factor_c: float32 [12, 128], replicated, may hold values from -1.75 to 1.75
Outputs:
- a_update: float32 [8192, 128], P(('row', 'col'))
- b_update: float32 [8192, 128], P(('col', 'row'))
The draws below stay inside these ranges and needn't reach their ends.
All inputs are finite; a program needn't handle non-finite values.
Results may differ from the reference program's by a relative error of at most 0.00012.
Values sent between devices are 32-bit elements; how exact they have to be, the bound alone decides.
No kernel may reach another device: no remote copies, remote signals or barrier semaphores. Data moves between devices by JAX's collectives and lax.ppermute only.
A program may use at most 64 MiB of HBM per device.

```python
import jax
import jax.numpy as jnp
from jax import lax

K = 12
R = 128
I = 8192
J = 8192


def raised(array, key, source, target, blocks, factor):
    owner, partner = [(jnp.arange(array.shape[dim]) // (array.shape[dim] // blocks)).reshape([-1 if axis == dim else 1 for axis in range(array.ndim)]) for dim in (source, target)]
    chosen = jax.random.permutation(key, blocks)[partner]
    strong = (owner == chosen) | (owner == (partner + blocks // 2) % blocks)
    return jnp.where(strong, factor * array, array)


def level_of(rng, dims, pieces, smallest, high):
    gain, own = 1.0, jax.random.fold_in(rng, 6)
    for position, blocks in pieces:
        steps = jnp.exp(jax.random.uniform(jax.random.fold_in(own, position), (blocks,), jnp.float32, smallest / len(pieces), high / len(pieces)))
        gain = gain * jnp.repeat(steps, dims[position] // blocks).reshape([-1 if axis == position else 1 for axis in range(len(dims))])
    return gain


def noise(rng, extent, spread, reach, shards=(), kind=jnp.bfloat16):
    loudness = level_of(rng, extent, shards, -0.22, 0.18) if shards else 1.0
    entries = jax.random.normal(rng, extent, jnp.float32) * spread * loudness
    return jnp.minimum(jnp.maximum(entries, -reach), reach).astype(kind)


def gaussian_with(own_key, shape, spread, most, split, heavy, held_as=jnp.bfloat16):
    array = spread * jax.random.normal(own_key, shape, jnp.float32)
    if split:
        array = array * level_of(own_key, shape, split, -0.22, 0.18)
    return jnp.clip(raised(array, jax.random.fold_in(own_key, 3), *heavy), -most, most).astype(held_as)


def setup_inputs(seed: int = 0) -> dict:
    seeds = jax.random.split(jax.random.key(seed), 4)
    return {
        "tensor": gaussian_with(seeds[0], (K, I, J), 1.0, 6.0, ((1, 16), (2, 16)), (2, 1, 16, 2.0), jnp.float32),
        "factor_b": noise(seeds[1], (J, R), J ** -0.5, 0.0625, ((0, 256),), jnp.float32),
        "factor_c": noise(seeds[2], (K, R), K ** -0.5, 1.75, (), jnp.float32),
    }


EPSILON = 1e-06

def solve_system(rhs, system):
    highest = lax.Precision.HIGHEST
    lower = jnp.linalg.cholesky(system)
    inverse = jax.scipy.linalg.cho_solve((lower, True), jnp.eye(system.shape[0], dtype=system.dtype))
    return jnp.dot(rhs, inverse, precision=highest)

def reference(tensor, factor_b, factor_c):
    highest = lax.Precision.HIGHEST
    c_gram = jnp.dot(factor_c.T, factor_c, precision=highest)
    system_a = c_gram * jnp.dot(factor_b.T, factor_b, precision=highest)

    def mode_one(index, total):
        plane = lax.dynamic_index_in_dim(tensor, index, 0, keepdims=False)
        weights = factor_b * lax.dynamic_index_in_dim(factor_c, index, 0, keepdims=False)
        return total + jnp.dot(plane, weights, precision=highest)
    mttkrp_a = lax.fori_loop(0, K, mode_one, jnp.zeros((I, R), jnp.float32))
    a_update = solve_system(mttkrp_a, system_a)
    column_norm = jnp.sqrt(lax.optimization_barrier(jnp.sum(a_update * a_update, axis=0)) + EPSILON)
    factor_a = a_update / column_norm
    system_b = c_gram * jnp.dot(factor_a.T, factor_a, precision=highest)

    def mode_two(index, total):
        plane = lax.dynamic_index_in_dim(tensor, index, 0, keepdims=False)
        weights = factor_a * lax.dynamic_index_in_dim(factor_c, index, 0, keepdims=False)
        return total + jnp.dot(plane.T, weights, precision=highest)
    mttkrp_b = lax.fori_loop(0, K, mode_two, jnp.zeros((J, R), jnp.float32))
    b_update = solve_system(mttkrp_b, system_b)
    return (a_update, b_update)
```

```python
import functools

import jax
import jax.numpy as jnp
from jax import lax
from jax.experimental import pallas as pl
from jax.experimental.pallas import tpu as pltpu
from jax.sharding import Mesh
from jax.sharding import PartitionSpec as P

EPSILON = 1e-06
HIGHEST = lax.Precision.HIGHEST
VMEM = pl.BlockSpec(memory_space=pltpu.VMEM)
ANY = pl.BlockSpec(memory_space=pl.ANY)
SMEM = pl.BlockSpec(memory_space=pltpu.SMEM)
ROW = ("z", "core")
COL = ("x", "y")


def split(value):
    high = value.astype(jnp.bfloat16)
    low = (value - high.astype(jnp.float32)).astype(jnp.bfloat16)
    return high, low


def contract_rows(left, right):
    return lax.dot_general(
        left, right, (((0,), (0,)), ((), ())), precision=HIGHEST,
        preferred_element_type=jnp.float32,
    )


def dot32(left, right):
    return lax.dot_general(
        left, right, (((1,), (0,)), ((), ())), precision=HIGHEST,
        preferred_element_type=jnp.float32,
    )


def inverse(system):
    size = system.shape[0]
    lanes = lax.broadcasted_iota(jnp.int32, (1, size), 1)
    rows = lax.broadcasted_iota(jnp.int32, (size, 1), 0)
    matrix = system
    for k in range(size):
        pivot = 1.0 / matrix[k : k + 1, k : k + 1]
        row = jnp.where(lanes == k, pivot, matrix[k : k + 1, :] * pivot)
        column = jnp.where(rows == k, 0.0, matrix[:, k : k + 1])
        kept = jnp.where(lanes == k, 0.0, matrix)
        matrix = jnp.where(rows == k, row, kept - column * row)
    return matrix


def first_kernel(t_hbm, b_ref, c_ref, out_ref, t_buf, b_both, total, sems):
    slices = t_hbm.shape[0]
    for k in range(slices):
        pltpu.make_async_copy(t_hbm.at[k], t_buf.at[k], sems.at[k]).start()
    factor = b_ref[...]
    width = factor.shape[1]
    b_high, b_low = split(factor)
    b_both[:, :width] = b_high
    b_both[:, width:] = b_low
    gram = contract_rows(factor, factor)
    parts, rows, _ = out_ref.shape
    share = width // parts
    out_ref[:, rows - share :, :] = gram.reshape(parts, share, width)
    for k in range(slices):
        pltpu.make_async_copy(t_hbm.at[k], t_buf.at[k], sems.at[k]).wait()
        t_high, t_low = split(t_buf[k])
        main = jnp.dot(t_high, b_both[...], preferred_element_type=jnp.float32)
        rest = jnp.dot(t_low, b_both[:, :width], preferred_element_type=jnp.float32)
        term = (main[:, :width] + (main[:, width:] + rest)) * c_ref[k : k + 1, :]
        if k == 0:
            total[...] = term
        else:
            total[...] += term
    out_ref[:, : rows - share, :] = total[...].reshape(parts, rows - share, width)


def middle_kernel(where_ref, g_ref, c_ref, a_ref, scaled_ref, message_ref, block):
    parts, rows, width = g_ref.shape
    share = width // parts
    owned = rows - share
    factor_c = c_ref[...]
    system = contract_rows(factor_c, factor_c) * g_ref[:, owned:, :].reshape(width, width)
    solved = inverse(system)
    update = dot32(g_ref[:, :owned, :].reshape(parts * owned, width), solved)
    block[...] = update
    start = pl.multiple_of(where_ref[0] * owned, owned)
    a_ref[...] = block[pl.ds(start, owned), :]
    most = jnp.max(jnp.abs(update), axis=0, keepdims=True)
    most = jnp.where(most > 0.0, most, 1.0)
    scaled = update / most
    scaled_ref[...] = scaled
    gram = contract_rows(update, scaled)
    targets, height, _ = message_ref.shape
    piece = width // targets
    message_ref[:, :piece, :] = gram.reshape(targets, piece, width)
    message_ref[:, piece:, :] = jnp.broadcast_to(
        most.reshape(1, 1, width), (targets, height - piece, width)
    )


def second_kernel(t_hbm, scaled_ref, c_ref, out_ref, t_buf, total, sems):
    slices = t_hbm.shape[0]
    for k in range(slices):
        pltpu.make_async_copy(t_hbm.at[k], t_buf.at[k], sems.at[k]).start()
    turned = scaled_ref[...].T
    width = turned.shape[0]
    c_turned = c_ref[...].T
    for k in range(slices):
        w_high, w_low = split(turned * c_turned[:, k : k + 1])
        w_both = jnp.concatenate([w_high, w_low], axis=0)
        pltpu.make_async_copy(t_hbm.at[k], t_buf.at[k], sems.at[k]).wait()
        t_high, t_low = split(t_buf[k])
        main = jnp.dot(w_both, t_high, preferred_element_type=jnp.float32)
        rest = jnp.dot(w_high, t_low, preferred_element_type=jnp.float32)
        term = main[:width] + (main[width:] + rest)
        if k == 0:
            total[...] = term
        else:
            total[...] += term
    out_ref[...] = total[...].T.reshape(out_ref.shape)


def combine_kernel(message_ref, chunk_ref, scale_ref):
    senders, height, width = message_ref.shape
    piece = chunk_ref.shape[0]
    all_most = message_ref[:, piece, :]
    most = jnp.max(all_most, axis=0, keepdims=True)
    scales = all_most / most
    chunk = jnp.zeros(chunk_ref.shape, jnp.float32)
    for d in range(senders):
        chunk += message_ref[d, :piece, :] * scales[d : d + 1, :]
    chunk_ref[...] = chunk
    scale_ref[:senders, :] = scales
    scale_ref[senders:, :] = jnp.broadcast_to(most, (scale_ref.shape[0] - senders, width))


def last_kernel(parts_ref, h_ref, scale_ref, c_ref, out_ref):
    senders, owned, width = parts_ref.shape
    scales = scale_ref[:senders, :]
    most = scale_ref[senders : senders + 1, :]
    total = jnp.zeros((owned, width), jnp.float32)
    for d in range(senders):
        total += parts_ref[d] * scales[d : d + 1, :]
    gram = h_ref[...].reshape(width, width)
    same = lax.broadcasted_iota(jnp.int32, (width, width), 0) == lax.broadcasted_iota(
        jnp.int32, (width, width), 1
    )
    norms = jnp.sqrt(jnp.sum(jnp.where(same, gram, 0.0), axis=0, keepdims=True) * most + EPSILON)
    ratio = most / norms
    flipped = jnp.sum(jnp.where(same, jnp.broadcast_to(norms, (width, width)), 0.0), axis=1, keepdims=True)
    factor_c = c_ref[...]
    system = contract_rows(factor_c, factor_c) * ((gram * ratio) / flipped)
    out_ref[...] = dot32(total * ratio, inverse(system))


def per_device(tensor, factor_b, factor_c):
    slices, rows_block, cols_block = tensor.shape
    width = factor_c.shape[1]
    row_size = lax.axis_size(ROW)
    col_size = lax.axis_size(COL)
    owned_a = rows_block // col_size
    owned_b = cols_block // row_size
    share_a = width // col_size
    share_b = width // row_size
    f32 = jnp.float32
    params = pltpu.CompilerParams(vmem_limit_bytes=48 * 1024 * 1024)

    b_block = lax.all_gather(factor_b, ROW, axis=0, tiled=True)
    packed = pl.pallas_call(
        first_kernel,
        out_shape=jax.ShapeDtypeStruct((col_size, owned_a + share_a, width), f32),
        in_specs=[ANY, VMEM, VMEM],
        out_specs=VMEM,
        scratch_shapes=[
            pltpu.VMEM((slices, rows_block, cols_block), f32),
            pltpu.VMEM((cols_block, 2 * width), jnp.bfloat16),
            pltpu.VMEM((rows_block, width), f32),
            pltpu.SemaphoreType.DMA((slices,)),
        ],
        compiler_params=params,
        name="first",
    )(tensor, b_block, factor_c)
    received = lax.all_to_all(packed, COL, 0, 0, tiled=True)
    summed = jnp.sum(received, axis=0)
    gathered = lax.all_to_all(
        jnp.broadcast_to(summed[None], received.shape), COL, 0, 0, tiled=True
    )
    where = lax.axis_index(COL).astype(jnp.int32).reshape(1)
    a_update, scaled, message = pl.pallas_call(
        middle_kernel,
        out_shape=(
            jax.ShapeDtypeStruct((owned_a, width), f32),
            jax.ShapeDtypeStruct((rows_block, width), f32),
            jax.ShapeDtypeStruct((row_size, share_b + 8, width), f32),
        ),
        in_specs=[SMEM, VMEM, VMEM],
        out_specs=(VMEM, VMEM, VMEM),
        scratch_shapes=[pltpu.VMEM((rows_block, width), f32)],
        name="middle",
    )(where, gathered, factor_c)
    grams = lax.all_to_all(message, ROW, 0, 0, tiled=True)
    partial_b = pl.pallas_call(
        second_kernel,
        out_shape=jax.ShapeDtypeStruct((row_size, owned_b, width), f32),
        in_specs=[ANY, VMEM, VMEM],
        out_specs=VMEM,
        scratch_shapes=[
            pltpu.VMEM((slices, rows_block, cols_block), f32),
            pltpu.VMEM((width, cols_block), f32),
            pltpu.SemaphoreType.DMA((slices,)),
        ],
        compiler_params=params,
        cost_estimate=pl.CostEstimate(
            flops=6 * slices * rows_block * cols_block * width,
            bytes_accessed=4 * slices * rows_block * cols_block,
            transcendentals=0,
        ),
        name="second",
    )(tensor, scaled, factor_c)
    chunk, scales = pl.pallas_call(
        combine_kernel,
        out_shape=(
            jax.ShapeDtypeStruct((share_b, width), f32),
            jax.ShapeDtypeStruct((row_size + 8, width), f32),
        ),
        in_specs=[VMEM],
        out_specs=(VMEM, VMEM),
        name="combine",
    )(grams)
    outgoing = jnp.concatenate(
        [partial_b, jnp.broadcast_to(chunk[None], (row_size,) + chunk.shape)], axis=1
    )
    final = lax.all_to_all(outgoing, ROW, 0, 0, tiled=True)
    b_update = pl.pallas_call(
        last_kernel,
        out_shape=jax.ShapeDtypeStruct((owned_b, width), f32),
        in_specs=[VMEM] * 4,
        out_specs=VMEM,
        name="last",
    )(final[:, :owned_b, :], final[:, owned_b:, :], scales, factor_c)
    return (a_update, b_update)


def solution(mesh):
    finer = Mesh(mesh.devices.reshape(8, 2, 4, 4), ("z", "core", "x", "y"))
    placed = (P(None, ROW, COL), P(COL + ROW, None), P())
    return jax.shard_map(
        per_device,
        mesh=finer,
        in_specs=placed,
        out_specs=(P(ROW + COL, None), P(COL + ROW, None)),
        check_vma=False,
    )
```

```python
import jax
import jax.numpy as jnp
from jax import lax
from jax.experimental import pallas as pl
from jax.experimental.pallas import tpu as pltpu
from jax.sharding import Mesh
from jax.sharding import PartitionSpec as P

EPSILON = 1e-06
HIGHEST = lax.Precision.HIGHEST
VMEM = pl.BlockSpec(memory_space=pltpu.VMEM)
HBM = pl.BlockSpec(memory_space=pltpu.HBM)
SMEM = pl.BlockSpec(memory_space=pltpu.SMEM)
ROW = ("z", "core")
COL = ("x", "y")
LARGE_MIB = 52
WORK_MIB = 12


def split(value):
    high = value.astype(jnp.bfloat16)
    low = (value - high.astype(jnp.float32)).astype(jnp.bfloat16)
    return high, low


def contract_rows(left, right):
    return lax.dot_general(
        left, right, (((0,), (0,)), ((), ())), precision=HIGHEST,
        preferred_element_type=jnp.float32,
    )


def dot32(left, right):
    return lax.dot_general(
        left, right, (((1,), (0,)), ((), ())), precision=HIGHEST,
        preferred_element_type=jnp.float32,
    )


def inverse(system):
    size = system.shape[0]
    lane = lax.broadcasted_iota(jnp.int32, (8, size), 1)
    sublane = lax.broadcasted_iota(jnp.int32, (8, size), 0)

    def spread(value):
        return jnp.broadcast_to(value, (8, size))

    strips = [system[8 * i : 8 * i + 8, :] for i in range(size // 8)]
    for c in range(size // 8):
        first = 8 * c
        columns = [spread(strips[c][:, first + j : first + j + 1]) for j in range(8)]
        entry = {(i, j): spread(columns[j][i : i + 1, :]) for j in range(8) for i in range(j + 1)}

        def key(i, j):
            return (i, j) if i <= j else (j, i)

        for k in range(8):
            pivot = 1.0 / entry[k, k]
            old = [entry[key(i, k)] for i in range(8)]
            part = [value * pivot for value in old]
            for i in range(8):
                for j in range(i, 8):
                    if i != k and j != k:
                        entry[i, j] = entry[i, j] - part[i] * old[j]
            for i in range(8):
                entry[key(i, k)] = -pivot if i == k else part[i]
        inside = (lane >= first) & (lane < first + 8)
        rows = [
            jnp.where(
                inside,
                jnp.where(lane == first + j, 1.0, 0.0),
                spread(strips[c][j : j + 1, :]),
            )
            for j in range(8)
        ]
        minus = []
        for i in range(8):
            terms = [entry[key(i, j)] * rows[j] for j in range(8)]
            minus.append(
                ((terms[0] + terms[1]) + (terms[2] + terms[3]))
                + ((terms[4] + terms[5]) + (terms[6] + terms[7]))
            )
        for m in range(size // 8):
            if m == c:
                continue
            terms = [
                spread(strips[m][:, first + j : first + j + 1]) * minus[j] for j in range(8)
            ]
            strips[m] = jnp.where(inside, 0.0, strips[m]) + (
                ((terms[0] + terms[1]) + (terms[2] + terms[3]))
                + ((terms[4] + terms[5]) + (terms[6] + terms[7]))
            )
        solved = minus[0]
        for i in range(1, 8):
            solved = jnp.where(sublane == i, minus[i], solved)
        strips[c] = -solved
    return jnp.concatenate(strips, axis=0)


def first_kernel(core_ref, t_hbm, mine_ref, other_ref, c_ref, out_ref, t_buf, b_block, b_both, total, sems):
    slices = t_hbm.shape[0]
    for k in range(slices):
        pltpu.make_async_copy(t_hbm.at[k], t_buf.at[k], sems.at[k]).start()
    core = core_ref[0]
    b_block[:, core] = mine_ref[...]
    b_block[:, 1 - core] = other_ref[...]
    width = c_ref.shape[1]
    factor = b_block[...].reshape(b_both.shape[0], width)
    b_high, b_low = split(factor)
    b_both[:, :width] = b_high
    b_both[:, width:] = b_low
    gram = contract_rows(factor, factor)
    parts, rows, _ = out_ref.shape
    share = width // parts
    out_ref[:, rows - share :, :] = gram.reshape(parts, share, width)
    for k in range(slices):
        pltpu.make_async_copy(t_hbm.at[k], t_buf.at[k], sems.at[k]).wait()
        t_high, t_low = split(t_buf[k])
        main = jnp.dot(t_high, b_both[...], preferred_element_type=jnp.float32)
        rest = jnp.dot(t_low, b_both[:, :width], preferred_element_type=jnp.float32)
        term = (main[:, :width] + (main[:, width:] + rest)) * c_ref[k : k + 1, :]
        if k == 0:
            total[...] = term
        else:
            total[...] += term
    out_ref[:, : rows - share, :] = total[...].reshape(parts, rows - share, width)


def sum_kernel(in_ref, out_ref):
    parts = in_ref.shape[0]
    total = in_ref[0]
    for d in range(1, parts):
        total += in_ref[d]
    out_ref[...] = jnp.broadcast_to(total[None], out_ref.shape)


def middle_kernel(where_ref, g_ref, c_ref, a_ref, scaled_ref, message_ref, block):
    parts, rows, width = g_ref.shape
    share = width // parts
    owned = rows - share
    factor_c = c_ref[...]
    system = contract_rows(factor_c, factor_c) * g_ref[:, owned:, :].reshape(width, width)
    solved = inverse(system)
    update = dot32(g_ref[:, :owned, :].reshape(parts * owned, width), solved)
    block[...] = update
    start = pl.multiple_of(where_ref[0] * owned, owned)
    a_ref[...] = block[pl.ds(start, owned), :]
    most = jnp.max(jnp.abs(update), axis=0, keepdims=True)
    most = jnp.where(most > 0.0, most, 1.0)
    scaled = update / most
    scaled_ref[...] = scaled
    gram = contract_rows(update, scaled)
    targets, height, _ = message_ref.shape
    piece = width // targets
    message_ref[:, :piece, :] = gram.reshape(targets, piece, width)
    message_ref[:, piece:, :] = jnp.broadcast_to(
        most.reshape(1, 1, width), (targets, height - piece, width)
    )


def second_kernel(t_hbm, scaled_ref, c_ref, out_ref, t_buf, total, sems):
    slices = t_hbm.shape[0]
    for k in range(slices):
        pltpu.make_async_copy(t_hbm.at[k], t_buf.at[k], sems.at[k]).start()
    turned = scaled_ref[...].T
    width = turned.shape[0]
    c_turned = c_ref[...].T
    for k in range(slices):
        w_high, w_low = split(turned * c_turned[:, k : k + 1])
        w_both = jnp.concatenate([w_high, w_low], axis=0)
        pltpu.make_async_copy(t_hbm.at[k], t_buf.at[k], sems.at[k]).wait()
        t_high, t_low = split(t_buf[k])
        main = jnp.dot(w_both, t_high, preferred_element_type=jnp.float32)
        rest = jnp.dot(w_high, t_low, preferred_element_type=jnp.float32)
        term = main[:width] + (main[width:] + rest)
        if k == 0:
            total[...] = term
        else:
            total[...] += term
    out_ref[...] = total[...].T.reshape(out_ref.shape)


def combine_kernel(own_ref, message_ref, partial_ref, send_ref, keep_ref, chunk_ref, most_ref):
    senders, height, width = message_ref.shape
    piece = chunk_ref.shape[0]
    core = own_ref[1]
    most = jnp.max(message_ref[:, piece, :], axis=0, keepdims=True)
    chunk = jnp.zeros((piece, width), jnp.float32)
    for d in range(senders):
        chunk += message_ref[d, :piece, :] * (message_ref[d, piece : piece + 1, :] / most)
    scale = message_ref[own_ref[0], piece : piece + 1, :] / most
    halves = keep_ref.shape
    send_ref[: send_ref.shape[0] - piece, :] = (partial_ref[:, 1 - core] * scale).reshape(
        halves[0] * halves[1], width
    )
    send_ref[send_ref.shape[0] - piece :, :] = chunk
    keep_ref[...] = partial_ref[:, core] * scale
    chunk_ref[...] = chunk
    most_ref[...] = jnp.broadcast_to(most, most_ref.shape)


def pair_kernel(own_ref, keep_ref, chunk_ref, got_ref, out_ref, both):
    targets, owned, width = keep_ref.shape
    piece = chunk_ref.shape[0]
    core = own_ref[1]
    both[core] = chunk_ref[...]
    both[1 - core] = got_ref[targets * owned :, :]
    out_ref[:, :owned, :] = keep_ref[...] + got_ref[: targets * owned, :].reshape(keep_ref.shape)
    out_ref[:, owned:, :] = jnp.broadcast_to(
        both[...].reshape(1, 2 * piece, width), (targets, 2 * piece, width)
    )


def last_kernel(parts_ref, most_ref, c_ref, out_ref):
    senders, height, width = parts_ref.shape
    owned = out_ref.shape[0]
    most = most_ref[:1, :]
    total = parts_ref[0, :owned, :]
    for d in range(1, senders):
        total += parts_ref[d, :owned, :]
    gram = parts_ref[:, owned:, :].reshape(width, width)
    same = lax.broadcasted_iota(jnp.int32, (width, width), 0) == lax.broadcasted_iota(
        jnp.int32, (width, width), 1
    )
    norms = jnp.sqrt(jnp.sum(jnp.where(same, gram, 0.0), axis=0, keepdims=True) * most + EPSILON)
    ratio = most / norms
    flipped = jnp.sum(jnp.where(same, jnp.broadcast_to(norms, (width, width)), 0.0), axis=1, keepdims=True)
    factor_c = c_ref[...]
    system = contract_rows(factor_c, factor_c) * ((gram * ratio) / flipped)
    out_ref[...] = dot32(total * ratio, inverse(system))


def limited(mebibytes):
    return pltpu.CompilerParams(vmem_limit_bytes=mebibytes * 1024 * 1024)


def per_device(tensor, factor_b, factor_c):
    slices, rows_block, cols_block = tensor.shape
    width = factor_c.shape[1]
    row_size = lax.axis_size(ROW)
    col_size = lax.axis_size(COL)
    z_size = lax.axis_size("z")
    owned_a = rows_block // col_size
    owned_b = cols_block // row_size
    share_a = width // col_size
    share_b = width // row_size
    f32 = jnp.float32
    shape = jax.ShapeDtypeStruct

    spread_b = jnp.broadcast_to(factor_b[None], (z_size,) + factor_b.shape)
    mine = lax.all_to_all(spread_b, "z", 0, 0, tiled=True)
    other = lax.ppermute(mine, "core", [(0, 1), (1, 0)])
    core = lax.axis_index("core").astype(jnp.int32).reshape(1)
    packed = pl.pallas_call(
        first_kernel,
        out_shape=shape((col_size, owned_a + share_a, width), f32),
        in_specs=[SMEM, HBM, VMEM, VMEM, VMEM],
        out_specs=VMEM,
        scratch_shapes=[
            pltpu.VMEM(tensor.shape, f32),
            pltpu.VMEM((z_size, 2, owned_b, width), f32),
            pltpu.VMEM((cols_block, 2 * width), jnp.bfloat16),
            pltpu.VMEM((rows_block, width), f32),
            pltpu.SemaphoreType.DMA((slices,)),
        ],
        compiler_params=limited(LARGE_MIB),
        name="first",
    )(core, tensor, mine, other, factor_c)
    received = lax.all_to_all(packed, COL, 0, 0, tiled=True)
    summed = pl.pallas_call(
        sum_kernel,
        out_shape=shape(received.shape, f32),
        in_specs=[VMEM],
        out_specs=VMEM,
        compiler_params=limited(WORK_MIB),
        name="sum",
    )(received)
    gathered = lax.all_to_all(summed, COL, 0, 0, tiled=True)
    where = lax.axis_index(COL).astype(jnp.int32).reshape(1)
    a_update, scaled, message = pl.pallas_call(
        middle_kernel,
        out_shape=(
            shape((owned_a, width), f32),
            shape((rows_block, width), f32),
            shape((row_size, share_b + 8, width), f32),
        ),
        in_specs=[SMEM, VMEM, VMEM],
        out_specs=(VMEM, VMEM, VMEM),
        scratch_shapes=[pltpu.VMEM((rows_block, width), f32)],
        compiler_params=limited(WORK_MIB),
        name="middle",
    )(where, gathered, factor_c)
    grams = lax.all_to_all(message, ROW, 0, 0, tiled=True)
    partial_b = pl.pallas_call(
        second_kernel,
        out_shape=shape((row_size, owned_b, width), f32),
        in_specs=[HBM, VMEM, VMEM],
        out_specs=VMEM,
        scratch_shapes=[
            pltpu.VMEM(tensor.shape, f32),
            pltpu.VMEM((width, cols_block), f32),
            pltpu.SemaphoreType.DMA((slices,)),
        ],
        compiler_params=limited(LARGE_MIB),
        cost_estimate=pl.CostEstimate(
            flops=6 * tensor.size * width, bytes_accessed=4 * tensor.size, transcendentals=0
        ),
        name="second",
    )(tensor, scaled, factor_c)
    own = jnp.stack([lax.axis_index(ROW), lax.axis_index("core")]).astype(jnp.int32)
    send, keep, chunk, most = pl.pallas_call(
        combine_kernel,
        out_shape=(
            shape((z_size * owned_b + share_b, width), f32),
            shape((z_size, owned_b, width), f32),
            shape((share_b, width), f32),
            shape((8, width), f32),
        ),
        in_specs=[SMEM, VMEM, VMEM],
        out_specs=(VMEM,) * 4,
        compiler_params=limited(WORK_MIB),
        name="combine",
    )(own, grams, partial_b.reshape(z_size, 2, owned_b, width))
    got = lax.ppermute(send, "core", [(0, 1), (1, 0)])
    outgoing = pl.pallas_call(
        pair_kernel,
        out_shape=shape((z_size, owned_b + 2 * share_b, width), f32),
        in_specs=[SMEM] + [VMEM] * 3,
        out_specs=VMEM,
        scratch_shapes=[pltpu.VMEM((2, share_b, width), f32)],
        compiler_params=limited(WORK_MIB),
        name="pair",
    )(own, keep, chunk, got)
    final = lax.all_to_all(outgoing, "z", 0, 0, tiled=True)
    b_update = pl.pallas_call(
        last_kernel,
        out_shape=shape((owned_b, width), f32),
        in_specs=[VMEM] * 3,
        out_specs=VMEM,
        compiler_params=limited(WORK_MIB),
        name="last",
    )(final, most, factor_c)
    return (a_update, b_update)


def solution(mesh):
    finer = Mesh(mesh.devices.reshape(8, 2, 4, 4), ("z", "core", "x", "y"))
    placed = (P(None, ROW, COL), P(COL + ROW, None), P())
    return jax.shard_map(
        per_device,
        mesh=finer,
        in_specs=placed,
        out_specs=(P(ROW + COL, None), P(COL + ROW, None)),
        check_vma=False,
    )
```

```python
import functools

import jax
import jax.numpy as jnp
from jax import lax
from jax.experimental import pallas as pl
from jax.experimental.pallas import tpu as pltpu
from jax.sharding import Mesh
from jax.sharding import PartitionSpec as P


EPSILON = 1e-06
HIGHEST = lax.Precision.HIGHEST
VMEM = pl.BlockSpec(memory_space=pltpu.VMEM)
HBM = pl.BlockSpec(memory_space=pltpu.HBM)
SMEM = pl.BlockSpec(memory_space=pltpu.SMEM)
ROW = ("z", "core")
COL = ("x", "y")
TINY = 1e-30
PARTS = 3
LARGE_MIB = 52
WORK_MIB = 12


def split(value):
    high = value.astype(jnp.bfloat16)
    low = (value - high.astype(jnp.float32)).astype(jnp.bfloat16)
    return high, low


def contract_rows(left, right):
    return lax.dot_general(
        left, right, (((0,), (0,)), ((), ())), precision=HIGHEST,
        preferred_element_type=jnp.float32,
    )


def dot32(left, right):
    return lax.dot_general(
        left, right, (((1,), (0,)), ((), ())), precision=HIGHEST,
        preferred_element_type=jnp.float32,
    )


def inverse(system):
    size = system.shape[0]
    lane = lax.broadcasted_iota(jnp.int32, (8, size), 1)
    sublane = lax.broadcasted_iota(jnp.int32, (8, size), 0)

    def spread(value):
        return jnp.broadcast_to(value, (8, size))

    strips = [system[8 * i : 8 * i + 8, :] for i in range(size // 8)]
    for c in range(size // 8):
        first = 8 * c
        columns = [spread(strips[c][:, first + j : first + j + 1]) for j in range(8)]
        entry = {(i, j): spread(columns[j][i : i + 1, :]) for j in range(8) for i in range(j + 1)}

        def key(i, j):
            return (i, j) if i <= j else (j, i)

        for k in range(8):
            pivot = 1.0 / entry[k, k]
            old = [entry[key(i, k)] for i in range(8)]
            part = [value * pivot for value in old]
            for i in range(8):
                for j in range(i, 8):
                    if i != k and j != k:
                        entry[i, j] = entry[i, j] - part[i] * old[j]
            for i in range(8):
                entry[key(i, k)] = -pivot if i == k else part[i]
        inside = (lane >= first) & (lane < first + 8)
        rows = [
            jnp.where(
                inside,
                jnp.where(lane == first + j, 1.0, 0.0),
                spread(strips[c][j : j + 1, :]),
            )
            for j in range(8)
        ]
        minus = []
        for i in range(8):
            terms = [entry[key(i, j)] * rows[j] for j in range(8)]
            minus.append(
                ((terms[0] + terms[1]) + (terms[2] + terms[3]))
                + ((terms[4] + terms[5]) + (terms[6] + terms[7]))
            )
        for m in range(size // 8):
            if m == c:
                continue
            terms = [
                spread(strips[m][:, first + j : first + j + 1]) * minus[j] for j in range(8)
            ]
            strips[m] = jnp.where(inside, 0.0, strips[m]) + (
                ((terms[0] + terms[1]) + (terms[2] + terms[3]))
                + ((terms[4] + terms[5]) + (terms[6] + terms[7]))
            )
        solved = minus[0]
        for i in range(1, 8):
            solved = jnp.where(sublane == i, minus[i], solved)
        strips[c] = -solved
    return jnp.concatenate(strips, axis=0)


def first_kernel(core_ref, t_hbm, mine_ref, other_ref, c_hbm, out_ref, t_buf, b_block, b_both, total, c_ref, sems):
    slices = t_hbm.shape[0]
    pltpu.make_async_copy(c_hbm, c_ref, sems.at[slices]).start()
    for k in range(slices):
        pltpu.make_async_copy(t_hbm.at[k], t_buf.at[k], sems.at[k]).start()
    core = core_ref[0]
    b_block[:, core] = mine_ref[...]
    b_block[:, 1 - core] = other_ref[...]
    width = c_ref.shape[1]
    factor = b_block[...].reshape(b_both.shape[0], width)
    b_high, b_low = split(factor)
    b_both[:, :width] = b_high
    b_both[:, width:] = b_low
    gram = contract_rows(factor, factor)
    parts, rows, _ = out_ref.shape
    share = width // parts
    out_ref[:, rows - share :, :] = gram.reshape(parts, share, width)
    pltpu.make_async_copy(c_hbm, c_ref, sems.at[slices]).wait()
    for k in range(slices):
        pltpu.make_async_copy(t_hbm.at[k], t_buf.at[k], sems.at[k]).wait()
        t_high, t_low = split(t_buf[k])
        main = jnp.dot(t_high, b_both[...], preferred_element_type=jnp.float32)
        rest = jnp.dot(t_low, b_both[:, :width], preferred_element_type=jnp.float32)
        term = (main[:, :width] + (main[:, width:] + rest)) * c_ref[k : k + 1, :]
        if k == 0:
            total[...] = term
        else:
            total[...] += term
    out_ref[:, : rows - share, :] = total[...].reshape(parts, rows - share, width)


def sum_kernel(in_ref, out_ref):
    parts = in_ref.shape[0]
    total = in_ref[0]
    for d in range(1, parts):
        total += in_ref[d]
    out_ref[...] = jnp.broadcast_to(total[None], out_ref.shape)


def middle_kernel(where_ref, g_ref, c_ref, a_ref, scaled_ref, message_ref, block):
    parts, rows, width = g_ref.shape
    share = width // parts
    owned = rows - share
    factor_c = c_ref[...]
    system = contract_rows(factor_c, factor_c) * g_ref[:, owned:, :].reshape(width, width)
    solved = inverse(system)
    update = dot32(g_ref[:, :owned, :].reshape(parts * owned, width), solved)
    block[...] = update
    start = pl.multiple_of(where_ref[0] * owned, owned)
    a_ref[...] = block[pl.ds(start, owned), :]
    most = jnp.max(jnp.abs(update), axis=0, keepdims=True)
    most = jnp.where(most > 0.0, most, TINY)
    scaled = update / most
    scaled_ref[...] = scaled
    message_ref[:width, :] = contract_rows(update, scaled)
    message_ref[width:, :] = jnp.broadcast_to(most, (message_ref.shape[0] - width, width))


def merge(mine_ref, got_ref):
    width = mine_ref.shape[1]
    mine = mine_ref[width : width + 1, :]
    got = got_ref[width : width + 1, :]
    most = jnp.maximum(mine, got)
    return mine_ref[:width, :] * (mine / most) + got_ref[:width, :] * (got / most), most


def merge_kernel(mine_ref, got_ref, out_ref):
    gram, most = merge(mine_ref, got_ref)
    width = gram.shape[1]
    out_ref[:width, :] = gram
    out_ref[width:, :] = jnp.broadcast_to(most, (out_ref.shape[0] - width, width))


def partial_sum(begin, t_hbm, scaled_ref, c_ref, total, t_buf, sems, fresh):
    slices = t_buf.shape[0]
    for k in range(slices):
        pltpu.make_async_copy(t_hbm.at[begin + k], t_buf.at[k], sems.at[k]).start()
    turned = scaled_ref[...].T
    width = turned.shape[0]
    c_turned = c_ref[...].T
    for k in range(slices):
        w_high, w_low = split(turned * c_turned[:, begin + k : begin + k + 1])
        w_both = jnp.concatenate([w_high, w_low], axis=0)
        pltpu.make_async_copy(t_hbm.at[begin + k], t_buf.at[k], sems.at[k]).wait()
        t_high, t_low = split(t_buf[k])
        main = jnp.dot(w_both, t_high, preferred_element_type=jnp.float32)
        rest = jnp.dot(w_high, t_low, preferred_element_type=jnp.float32)
        term = main[:width] + (main[width:] + rest)
        if fresh and k == 0:
            total[...] = term
        else:
            total[...] += term


def head_kernel(begin, t_hbm, scaled_ref, c_ref, out_ref, t_buf, sems):
    partial_sum(begin, t_hbm, scaled_ref, c_ref, out_ref, t_buf, sems, True)


def body_kernel(begin, t_hbm, scaled_ref, c_ref, in_ref, out_ref, t_buf, sems):
    out_ref[...] = in_ref[...]
    partial_sum(begin, t_hbm, scaled_ref, c_ref, out_ref, t_buf, sems, False)


def tail_kernel(begin, core_ref, t_hbm, scaled_ref, c_ref, in_ref, message_ref, pair_ref, send_ref, keep_ref, total, halves, t_buf, sems):
    total[...] = in_ref[...]
    partial_sum(begin, t_hbm, scaled_ref, c_ref, total, t_buf, sems, False)
    width = scaled_ref.shape[1]
    scale = message_ref[width : width + 1, :] / pair_ref[width : width + 1, :]
    halves[...] = (total[...].T * scale).reshape(halves.shape)
    core = core_ref[0]
    send_ref[...] = halves[:, 1 - core].reshape(send_ref.shape)
    keep_ref[...] = halves[:, core]


def pair_kernel(keep_ref, got_ref, pair_ref, out_ref):
    targets, owned, width = keep_ref.shape
    out_ref[:, :owned, :] = keep_ref[...] + got_ref[...].reshape(keep_ref.shape)
    out_ref[:, owned:, :] = jnp.broadcast_to(
        pair_ref[width : width + 1, :].reshape(1, 1, width),
        (targets, out_ref.shape[1] - owned, width),
    )


def solve_kernel(mine_ref, got_ref, c_ref, out_ref):
    gram, most = merge(mine_ref, got_ref)
    width = gram.shape[1]
    same = lax.broadcasted_iota(jnp.int32, (width, width), 0) == lax.broadcasted_iota(
        jnp.int32, (width, width), 1
    )
    norms = jnp.sqrt(jnp.sum(jnp.where(same, gram, 0.0), axis=0, keepdims=True) * most + EPSILON)
    flipped = jnp.sum(jnp.where(same, jnp.broadcast_to(norms, (width, width)), 0.0), axis=1, keepdims=True)
    factor_c = c_ref[...]
    system = contract_rows(factor_c, factor_c) * ((gram * (most / norms)) / flipped)
    out_ref[:width, :] = inverse(system)
    out_ref[width:, :] = jnp.broadcast_to(norms, (out_ref.shape[0] - width, width))


def last_kernel(parts_ref, solved_ref, out_ref):
    senders, _, width = parts_ref.shape
    owned = out_ref.shape[0]
    norms = solved_ref[width : width + 1, :]
    total = jnp.zeros((owned, width), jnp.float32)
    for d in range(senders):
        total += parts_ref[d, :owned, :] * (parts_ref[d, owned : owned + 1, :] / norms)
    out_ref[...] = dot32(total, solved_ref[:width, :])


def limited(mebibytes):
    return pltpu.CompilerParams(vmem_limit_bytes=mebibytes * 1024 * 1024)


def per_device(tensor, factor_b, factor_c):
    slices, rows_block, cols_block = tensor.shape
    width = factor_c.shape[1]
    row_size = lax.axis_size(ROW)
    col_size = lax.axis_size(COL)
    z_size = lax.axis_size("z")
    owned_a = rows_block // col_size
    owned_b = cols_block // row_size
    share_a = width // col_size
    f32 = jnp.float32
    shape = jax.ShapeDtypeStruct

    spread_b = jnp.broadcast_to(factor_b[None], (z_size,) + factor_b.shape)
    mine = lax.all_to_all(spread_b, "z", 0, 0, tiled=True)
    other = lax.ppermute(mine, "core", [(0, 1), (1, 0)])
    core = lax.axis_index("core").astype(jnp.int32).reshape(1)
    packed = pl.pallas_call(
        first_kernel,
        out_shape=shape((col_size, owned_a + share_a, width), f32),
        in_specs=[SMEM, HBM, VMEM, VMEM, HBM],
        out_specs=VMEM,
        scratch_shapes=[
            pltpu.VMEM(tensor.shape, f32),
            pltpu.VMEM((z_size, 2, owned_b, width), f32),
            pltpu.VMEM((cols_block, 2 * width), jnp.bfloat16),
            pltpu.VMEM((rows_block, width), f32),
            pltpu.VMEM(factor_c.shape, f32),
            pltpu.SemaphoreType.DMA((slices + 1,)),
        ],
        compiler_params=limited(LARGE_MIB),
        name="first",
    )(core, tensor, mine, other, factor_c)
    received = lax.all_to_all(packed, COL, 0, 0, tiled=True)
    summed = pl.pallas_call(
        sum_kernel,
        out_shape=shape(received.shape, f32),
        in_specs=[VMEM],
        out_specs=VMEM,
        compiler_params=limited(WORK_MIB),
        name="sum",
    )(received)
    gathered = lax.all_to_all(summed, COL, 0, 0, tiled=True)
    where = lax.axis_index(COL).astype(jnp.int32).reshape(1)
    a_update, scaled, message = pl.pallas_call(
        middle_kernel,
        out_shape=(
            shape((owned_a, width), f32),
            shape((rows_block, width), f32),
            shape((width + 8, width), f32),
        ),
        in_specs=[SMEM, VMEM, VMEM],
        out_specs=(VMEM, VMEM, VMEM),
        scratch_shapes=[pltpu.VMEM((rows_block, width), f32)],
        compiler_params=limited(WORK_MIB),
        name="middle",
    )(where, gathered, factor_c)
    small = limited(WORK_MIB)
    swap = [(0, 1), (1, 0)]
    per_part = slices // PARTS
    part_cost = pl.CostEstimate(
        flops=6 * tensor.size * width // PARTS,
        bytes_accessed=4 * tensor.size // PARTS,
        transcendentals=0,
    )
    part_scratch = [
        pltpu.VMEM((per_part, rows_block, cols_block), f32),
        pltpu.SemaphoreType.DMA((per_part,)),
    ]
    running = shape((width, cols_block), f32)

    def merged(mine, got):
        return pl.pallas_call(
            merge_kernel,
            out_shape=shape(message.shape, f32),
            in_specs=[VMEM, VMEM],
            out_specs=VMEM,
            compiler_params=small,
            name="merge",
        )(mine, got)

    def flipped(array, distance):
        return lax.ppermute(array, "z", [(i, i ^ distance) for i in range(z_size)])

    got = lax.ppermute(message, "core", swap)
    total = pl.pallas_call(
        functools.partial(head_kernel, 0),
        out_shape=running,
        in_specs=[HBM, VMEM, VMEM],
        out_specs=VMEM,
        scratch_shapes=part_scratch,
        compiler_params=limited(LARGE_MIB),
        cost_estimate=part_cost,
        name="head",
    )(tensor, scaled, factor_c)
    pair = merged(message, got)
    got = flipped(pair, 1)
    total = pl.pallas_call(
        functools.partial(body_kernel, per_part),
        out_shape=running,
        in_specs=[HBM, VMEM, VMEM, VMEM],
        out_specs=VMEM,
        scratch_shapes=part_scratch,
        compiler_params=limited(LARGE_MIB),
        cost_estimate=part_cost,
        name="body",
    )(tensor, scaled, factor_c, total)
    quad = merged(pair, got)
    got = flipped(quad, 2)
    send, keep = pl.pallas_call(
        functools.partial(tail_kernel, 2 * per_part),
        out_shape=(
            shape((z_size * owned_b, width), f32),
            shape((z_size, owned_b, width), f32),
        ),
        in_specs=[SMEM, HBM] + [VMEM] * 5,
        out_specs=(VMEM, VMEM),
        scratch_shapes=[
            pltpu.VMEM((width, cols_block), f32),
            pltpu.VMEM((z_size, 2, owned_b, width), f32),
        ]
        + part_scratch,
        compiler_params=limited(LARGE_MIB),
        cost_estimate=part_cost,
        name="tail",
    )(core, tensor, scaled, factor_c, total, message, pair)
    octet = merged(quad, got)
    other_half = lax.ppermute(send, "core", swap)
    got = flipped(octet, 4)
    outgoing = pl.pallas_call(
        pair_kernel,
        out_shape=shape((z_size, owned_b + 8, width), f32),
        in_specs=[VMEM] * 3,
        out_specs=VMEM,
        compiler_params=small,
        name="pair",
    )(keep, other_half, pair)
    final = lax.all_to_all(outgoing, "z", 0, 0, tiled=True)
    solved = pl.pallas_call(
        solve_kernel,
        out_shape=shape(message.shape, f32),
        in_specs=[VMEM] * 3,
        out_specs=VMEM,
        compiler_params=small,
        cost_estimate=pl.CostEstimate(flops=10**9, bytes_accessed=10**6, transcendentals=0),
        name="solve",
    )(octet, got, factor_c)
    b_update = pl.pallas_call(
        last_kernel,
        out_shape=shape((owned_b, width), f32),
        in_specs=[VMEM, VMEM],
        out_specs=VMEM,
        compiler_params=small,
        name="last",
    )(final, solved)
    return (a_update, b_update)


def solution(mesh):
    finer = Mesh(mesh.devices.reshape(8, 2, 4, 4), ("z", "core", "x", "y"))
    placed = (P(None, ROW, COL), P(COL + ROW, None), P())

    return jax.shard_map(
        per_device,
        mesh=finer,
        in_specs=placed,
        out_specs=(P(ROW + COL, None), P(COL + ROW, None)),
        check_vma=False,
    )
```

```python
import functools

import jax
import jax.numpy as jnp
from jax import lax
from jax.experimental import pallas as pl
from jax.experimental.pallas import tpu as pltpu
from jax.sharding import Mesh
from jax.sharding import PartitionSpec as P


EPSILON = 1e-06
HIGHEST = lax.Precision.HIGHEST
VMEM = pl.BlockSpec(memory_space=pltpu.VMEM)
HBM = pl.BlockSpec(memory_space=pltpu.HBM)
SMEM = pl.BlockSpec(memory_space=pltpu.SMEM)
ROW = ("z", "core")
COL = ("x", "y")
TINY = 1e-30
HEAD = 3
LARGE_MIB = 52
WORK_MIB = 12


def split(value):
    high = value.astype(jnp.bfloat16)
    low = (value - high.astype(jnp.float32)).astype(jnp.bfloat16)
    return high, low


def contract_rows(left, right):
    return lax.dot_general(
        left, right, (((0,), (0,)), ((), ())), precision=HIGHEST,
        preferred_element_type=jnp.float32,
    )


def dot32(left, right):
    return lax.dot_general(
        left, right, (((1,), (0,)), ((), ())), precision=HIGHEST,
        preferred_element_type=jnp.float32,
    )


def dot_turned(left, right):
    return lax.dot_general(
        left, right, (((1,), (1,)), ((), ())), preferred_element_type=jnp.float32
    )


def inverse(system):
    size = system.shape[0]
    lane = lax.broadcasted_iota(jnp.int32, (8, size), 1)
    sublane = lax.broadcasted_iota(jnp.int32, (8, size), 0)

    def spread(value):
        return jnp.broadcast_to(value, (8, size))

    strips = [system[8 * i : 8 * i + 8, :] for i in range(size // 8)]
    for c in range(size // 8):
        first = 8 * c
        columns = [spread(strips[c][:, first + j : first + j + 1]) for j in range(8)]
        entry = {(i, j): spread(columns[j][i : i + 1, :]) for j in range(8) for i in range(j + 1)}

        def key(i, j):
            return (i, j) if i <= j else (j, i)

        for k in range(8):
            pivot = 1.0 / entry[k, k]
            old = [entry[key(i, k)] for i in range(8)]
            part = [value * pivot for value in old]
            for i in range(8):
                for j in range(i, 8):
                    if i != k and j != k:
                        entry[i, j] = entry[i, j] - part[i] * old[j]
            for i in range(8):
                entry[key(i, k)] = -pivot if i == k else part[i]
        inside = (lane >= first) & (lane < first + 8)
        rows = [
            jnp.where(
                inside,
                jnp.where(lane == first + j, 1.0, 0.0),
                spread(strips[c][j : j + 1, :]),
            )
            for j in range(8)
        ]
        minus = []
        for i in range(8):
            terms = [entry[key(i, j)] * rows[j] for j in range(8)]
            minus.append(
                ((terms[0] + terms[1]) + (terms[2] + terms[3]))
                + ((terms[4] + terms[5]) + (terms[6] + terms[7]))
            )
        for m in range(size // 8):
            if m == c:
                continue
            terms = [
                spread(strips[m][:, first + j : first + j + 1]) * minus[j] for j in range(8)
            ]
            strips[m] = jnp.where(inside, 0.0, strips[m]) + (
                ((terms[0] + terms[1]) + (terms[2] + terms[3]))
                + ((terms[4] + terms[5]) + (terms[6] + terms[7]))
            )
        solved = minus[0]
        for i in range(1, 8):
            solved = jnp.where(sublane == i, minus[i], solved)
        strips[c] = -solved
    return jnp.concatenate(strips, axis=0)


def stage_kernel(in_ref, out_ref):
    out_ref[...] = in_ref[...]


def first_kernel(own_ref, t_hbm, mine_ref, other_ref, c_ref, out_ref, t_buf, b_block, total, sems):
    slices = t_hbm.shape[0]
    for k in range(slices):
        pltpu.make_async_copy(t_hbm.at[k], t_buf.at[k], sems.at[k]).start()
    core = own_ref[0]
    b_block[:, core] = mine_ref[...]
    b_block[:, 1 - core] = other_ref[...]
    width = c_ref.shape[1]
    factor = b_block[...].reshape(t_hbm.shape[2], width)
    gram = contract_rows(factor, factor)
    parts, rows, _ = out_ref.shape
    share = width // parts
    out_ref[:, rows - share :, :] = gram.reshape(parts, share, width)
    turned = factor.T
    c_turned = c_ref[...].T
    for k in range(slices):
        w_high, w_low = split(turned * c_turned[:, k : k + 1])
        w_both = jnp.concatenate([w_high, w_low], axis=0)
        pltpu.make_async_copy(t_hbm.at[k], t_buf.at[k], sems.at[k]).wait()
        t_high, t_low = split(t_buf[k])
        main = dot_turned(w_both, t_high)
        rest = dot_turned(w_high, t_low)
        term = main[:width] + (main[width:] + rest)
        if k == 0:
            total[...] = term
        else:
            total[...] += term
    out_ref[:, : rows - share, :] = total[...].T.reshape(parts, rows - share, width)


def sum_kernel(in_ref, out_ref):
    parts = in_ref.shape[0]
    total = in_ref[0]
    for d in range(1, parts):
        total += in_ref[d]
    out_ref[...] = jnp.broadcast_to(total[None], out_ref.shape)


def middle_kernel(own_ref, g_ref, c_ref, a_ref, scaled_ref, message_ref, block):
    parts, rows, width = g_ref.shape
    share = width // parts
    owned = rows - share
    factor_c = c_ref[...]
    system = contract_rows(factor_c, factor_c) * g_ref[:, owned:, :].reshape(width, width)
    solved = inverse(system)
    update = dot32(g_ref[:, :owned, :].reshape(parts * owned, width), solved)
    block[...] = update
    start = pl.multiple_of(own_ref[1] * owned, owned)
    a_ref[...] = block[pl.ds(start, owned), :]
    most = jnp.max(jnp.abs(update), axis=0, keepdims=True)
    most = jnp.where(most > 0.0, most, TINY)
    scaled = update / most
    scaled_ref[...] = scaled
    message_ref[:width, :] = contract_rows(update, scaled)
    message_ref[width:, :] = jnp.broadcast_to(most, (message_ref.shape[0] - width, width))


def merge(mine_ref, got_ref):
    width = mine_ref.shape[1]
    mine = mine_ref[width : width + 1, :]
    got = got_ref[width : width + 1, :]
    most = jnp.maximum(mine, got)
    return mine_ref[:width, :] * (mine / most) + got_ref[:width, :] * (got / most), most


def merge_kernel(mine_ref, got_ref, out_ref):
    gram, most = merge(mine_ref, got_ref)
    width = gram.shape[1]
    out_ref[:width, :] = gram
    out_ref[width:, :] = jnp.broadcast_to(most, (out_ref.shape[0] - width, width))


def partial_sum(begin, t_hbm, scaled_ref, c_ref, total, t_buf, sems, fresh):
    slices = t_buf.shape[0]
    for k in range(slices):
        pltpu.make_async_copy(t_hbm.at[begin + k], t_buf.at[k], sems.at[k]).start()
    turned = scaled_ref[...].T
    width = turned.shape[0]
    c_turned = c_ref[...].T
    for k in range(slices):
        w_high, w_low = split(turned * c_turned[:, begin + k : begin + k + 1])
        w_both = jnp.concatenate([w_high, w_low], axis=0)
        pltpu.make_async_copy(t_hbm.at[begin + k], t_buf.at[k], sems.at[k]).wait()
        t_high, t_low = split(t_buf[k])
        main = jnp.dot(w_both, t_high, preferred_element_type=jnp.float32)
        rest = jnp.dot(w_high, t_low, preferred_element_type=jnp.float32)
        term = main[:width] + (main[width:] + rest)
        if fresh and k == 0:
            total[...] = term
        else:
            total[...] += term


def head_kernel(begin, t_hbm, scaled_ref, c_ref, out_ref, t_buf, sems):
    partial_sum(begin, t_hbm, scaled_ref, c_ref, out_ref, t_buf, sems, True)


def tail_kernel(begin, own_ref, t_hbm, scaled_ref, c_ref, in_ref, message_ref, pair_ref, send_ref, keep_ref, total, halves, t_buf, sems):
    total[...] = in_ref[...]
    partial_sum(begin, t_hbm, scaled_ref, c_ref, total, t_buf, sems, False)
    width = scaled_ref.shape[1]
    scale = message_ref[width : width + 1, :] / pair_ref[width : width + 1, :]
    halves[...] = (total[...].T * scale).reshape(halves.shape)
    core = own_ref[0]
    send_ref[...] = halves[:, 1 - core].reshape(send_ref.shape)
    keep_ref[...] = halves[:, core]


def pair_kernel(keep_ref, got_ref, pair_ref, out_ref):
    targets, owned, width = keep_ref.shape
    out_ref[:, :owned, :] = keep_ref[...] + got_ref[...].reshape(keep_ref.shape)
    out_ref[:, owned:, :] = jnp.broadcast_to(
        pair_ref[width : width + 1, :].reshape(1, 1, width),
        (targets, out_ref.shape[1] - owned, width),
    )


def solve_kernel(mine_ref, got_ref, c_ref, out_ref):
    gram, most = merge(mine_ref, got_ref)
    width = gram.shape[1]
    same = lax.broadcasted_iota(jnp.int32, (width, width), 0) == lax.broadcasted_iota(
        jnp.int32, (width, width), 1
    )
    norms = jnp.sqrt(jnp.sum(jnp.where(same, gram, 0.0), axis=0, keepdims=True) * most + EPSILON)
    flipped = jnp.sum(jnp.where(same, jnp.broadcast_to(norms, (width, width)), 0.0), axis=1, keepdims=True)
    factor_c = c_ref[...]
    system = contract_rows(factor_c, factor_c) * ((gram * (most / norms)) / flipped)
    out_ref[:width, :] = inverse(system)
    out_ref[width:, :] = jnp.broadcast_to(norms, (out_ref.shape[0] - width, width))


def last_kernel(parts_ref, solved_ref, out_ref):
    senders, _, width = parts_ref.shape
    owned = out_ref.shape[0]
    norms = solved_ref[width : width + 1, :]
    total = jnp.zeros((owned, width), jnp.float32)
    for d in range(senders):
        total += parts_ref[d, :owned, :] * (parts_ref[d, owned : owned + 1, :] / norms)
    out_ref[...] = dot32(total, solved_ref[:width, :])


def limited(mebibytes):
    return pltpu.CompilerParams(vmem_limit_bytes=mebibytes * 1024 * 1024)


def per_device(tensor, factor_b, factor_c):
    slices, rows_block, cols_block = tensor.shape
    width = factor_c.shape[1]
    row_size = lax.axis_size(ROW)
    col_size = lax.axis_size(COL)
    z_size = lax.axis_size("z")
    owned_a = rows_block // col_size
    owned_b = cols_block // row_size
    share_a = width // col_size
    f32 = jnp.float32
    shape = jax.ShapeDtypeStruct

    small = limited(WORK_MIB)
    swap = [(0, 1), (1, 0)]
    own = jnp.stack([lax.axis_index("core"), lax.axis_index(COL)]).astype(jnp.int32)
    spread_b = jnp.broadcast_to(factor_b[None], (z_size,) + factor_b.shape)
    mine = lax.all_to_all(spread_b, "z", 0, 0, tiled=True)
    other = lax.ppermute(mine, "core", swap)
    staged_c = pl.pallas_call(
        stage_kernel,
        out_shape=pltpu.VMEM(factor_c.shape, f32),
        in_specs=[VMEM],
        out_specs=VMEM,
        compiler_params=small,
        name="stage",
    )(factor_c)
    packed = pl.pallas_call(
        first_kernel,
        out_shape=shape((col_size, owned_a + share_a, width), f32),
        in_specs=[SMEM, HBM, VMEM, VMEM, VMEM],
        out_specs=VMEM,
        scratch_shapes=[
            pltpu.VMEM(tensor.shape, f32),
            pltpu.VMEM((z_size, 2, owned_b, width), f32),
            pltpu.VMEM((width, rows_block), f32),
            pltpu.SemaphoreType.DMA((slices,)),
        ],
        compiler_params=limited(LARGE_MIB),
        name="first",
    )(own, tensor, mine, other, staged_c)
    received = lax.all_to_all(packed, COL, 0, 0, tiled=True)
    summed = pl.pallas_call(
        sum_kernel,
        out_shape=shape(received.shape, f32),
        in_specs=[VMEM],
        out_specs=VMEM,
        compiler_params=limited(WORK_MIB),
        name="sum",
    )(received)
    gathered = lax.all_to_all(summed, COL, 0, 0, tiled=True)
    a_update, scaled, message = pl.pallas_call(
        middle_kernel,
        out_shape=(
            shape((owned_a, width), f32),
            shape((rows_block, width), f32),
            shape((width + 8, width), f32),
        ),
        in_specs=[SMEM, VMEM, VMEM],
        out_specs=(VMEM, VMEM, VMEM),
        scratch_shapes=[pltpu.VMEM((rows_block, width), f32)],
        compiler_params=limited(WORK_MIB),
        name="middle",
    )(own, gathered, staged_c)
    running = shape((width, cols_block), f32)

    def cost(count):
        return pl.CostEstimate(
            flops=6 * rows_block * cols_block * width * count,
            bytes_accessed=4 * rows_block * cols_block * count,
            transcendentals=0,
        )

    def part_scratch(count):
        return [
            pltpu.VMEM((count, rows_block, cols_block), f32),
            pltpu.SemaphoreType.DMA((count,)),
        ]

    def merged(mine, got):
        return pl.pallas_call(
            merge_kernel,
            out_shape=shape(message.shape, f32),
            in_specs=[VMEM, VMEM],
            out_specs=VMEM,
            compiler_params=small,
            name="merge",
        )(mine, got)

    def flipped(array, distance):
        return lax.ppermute(array, "z", [(i, i ^ distance) for i in range(z_size)])

    got = lax.ppermute(message, "core", swap)
    total = pl.pallas_call(
        functools.partial(head_kernel, 0),
        out_shape=running,
        in_specs=[HBM, VMEM, VMEM],
        out_specs=VMEM,
        scratch_shapes=part_scratch(HEAD),
        compiler_params=limited(LARGE_MIB),
        cost_estimate=cost(HEAD),
        name="head",
    )(tensor, scaled, staged_c)
    pair = merged(message, got)
    got = flipped(pair, 4)
    send, keep = pl.pallas_call(
        functools.partial(tail_kernel, HEAD),
        out_shape=(
            shape((z_size * owned_b, width), f32),
            shape((z_size, owned_b, width), f32),
        ),
        in_specs=[SMEM, HBM] + [VMEM] * 5,
        out_specs=(VMEM, VMEM),
        scratch_shapes=[
            pltpu.VMEM((width, cols_block), f32),
            pltpu.VMEM((z_size, 2, owned_b, width), f32),
        ]
        + part_scratch(slices - HEAD),
        compiler_params=limited(LARGE_MIB),
        cost_estimate=cost(slices - HEAD),
        name="tail",
    )(own, tensor, scaled, staged_c, total, message, pair)
    quad = merged(pair, got)
    other_half = lax.ppermute(send, "core", swap)
    got = flipped(quad, 2)
    octet = merged(quad, got)
    got = flipped(octet, 1)
    outgoing = pl.pallas_call(
        pair_kernel,
        out_shape=shape((z_size, owned_b + 8, width), f32),
        in_specs=[VMEM] * 3,
        out_specs=VMEM,
        compiler_params=small,
        name="pair",
    )(keep, other_half, pair)
    final = lax.all_to_all(outgoing, "z", 0, 0, tiled=True)
    solved = pl.pallas_call(
        solve_kernel,
        out_shape=shape(message.shape, f32),
        in_specs=[VMEM] * 3,
        out_specs=VMEM,
        compiler_params=small,
        cost_estimate=pl.CostEstimate(flops=10**9, bytes_accessed=10**6, transcendentals=0),
        name="solve",
    )(octet, got, staged_c)
    b_update = pl.pallas_call(
        last_kernel,
        out_shape=shape((owned_b, width), f32),
        in_specs=[VMEM, VMEM],
        out_specs=VMEM,
        compiler_params=small,
        name="last",
    )(final, solved)
    return (a_update, b_update)


def solution(mesh):
    finer = Mesh(mesh.devices.reshape(8, 2, 4, 4), ("z", "core", "x", "y"))
    placed = (P(None, ROW, COL), P(COL + ROW, None), P())

    return jax.shard_map(
        per_device,
        mesh=finer,
        in_specs=placed,
        out_specs=(P(ROW + COL, None), P(COL + ROW, None)),
        check_vma=False,
    )
```

```python
import jax
import jax.numpy as jnp
from jax import lax
from jax.experimental import pallas as pl
from jax.experimental.pallas import tpu as pltpu
from jax.sharding import Mesh
from jax.sharding import PartitionSpec as P


EPSILON = 1e-06
HIGHEST = lax.Precision.HIGHEST
VMEM = pl.BlockSpec(memory_space=pltpu.VMEM)
HBM = pl.BlockSpec(memory_space=pltpu.HBM)
SMEM = pl.BlockSpec(memory_space=pltpu.SMEM)
ROW = ("z", "core")
COL = ("x", "y")
TINY = 1e-30
LARGE_MIB = 52
WORK_MIB = 12


def split(value):
    high = value.astype(jnp.bfloat16)
    low = (value - high.astype(jnp.float32)).astype(jnp.bfloat16)
    return high, low


def contract_rows(left, right):
    return lax.dot_general(
        left, right, (((0,), (0,)), ((), ())), precision=HIGHEST,
        preferred_element_type=jnp.float32,
    )


def dot32(left, right):
    return lax.dot_general(
        left, right, (((1,), (0,)), ((), ())), precision=HIGHEST,
        preferred_element_type=jnp.float32,
    )


def dot_turned(left, right):
    return lax.dot_general(
        left, right, (((1,), (1,)), ((), ())), preferred_element_type=jnp.float32
    )


def inverse(system):
    size = system.shape[0]
    lane = lax.broadcasted_iota(jnp.int32, (8, size), 1)
    sublane = lax.broadcasted_iota(jnp.int32, (8, size), 0)

    def spread(value):
        return jnp.broadcast_to(value, (8, size))

    strips = [system[8 * i : 8 * i + 8, :] for i in range(size // 8)]
    for c in range(size // 8):
        first = 8 * c
        columns = [spread(strips[c][:, first + j : first + j + 1]) for j in range(8)]
        entry = {(i, j): spread(columns[j][i : i + 1, :]) for j in range(8) for i in range(j + 1)}

        def key(i, j):
            return (i, j) if i <= j else (j, i)

        for k in range(8):
            pivot = 1.0 / entry[k, k]
            old = [entry[key(i, k)] for i in range(8)]
            part = [value * pivot for value in old]
            for i in range(8):
                for j in range(i, 8):
                    if i != k and j != k:
                        entry[i, j] = entry[i, j] - part[i] * old[j]
            for i in range(8):
                entry[key(i, k)] = -pivot if i == k else part[i]
        inside = (lane >= first) & (lane < first + 8)
        rows = [
            jnp.where(
                inside,
                jnp.where(lane == first + j, 1.0, 0.0),
                spread(strips[c][j : j + 1, :]),
            )
            for j in range(8)
        ]
        minus = []
        for i in range(8):
            terms = [entry[key(i, j)] * rows[j] for j in range(8)]
            minus.append(
                ((terms[0] + terms[1]) + (terms[2] + terms[3]))
                + ((terms[4] + terms[5]) + (terms[6] + terms[7]))
            )
        for m in range(size // 8):
            if m == c:
                continue
            terms = [
                spread(strips[m][:, first + j : first + j + 1]) * minus[j] for j in range(8)
            ]
            strips[m] = jnp.where(inside, 0.0, strips[m]) + (
                ((terms[0] + terms[1]) + (terms[2] + terms[3]))
                + ((terms[4] + terms[5]) + (terms[6] + terms[7]))
            )
        solved = minus[0]
        for i in range(1, 8):
            solved = jnp.where(sublane == i, minus[i], solved)
        strips[c] = -solved
    return jnp.concatenate(strips, axis=0)


def stage_kernel(in_ref, out_ref):
    out_ref[...] = in_ref[...]


def first_kernel(own_ref, t_hbm, mine_ref, other_ref, c_ref, out_ref, t_buf, b_block, total, sems):
    slices = t_hbm.shape[0]
    for k in range(slices):
        pltpu.make_async_copy(t_hbm.at[k], t_buf.at[k], sems.at[k]).start()
    core = own_ref[0]
    b_block[:, core] = mine_ref[...]
    b_block[:, 1 - core] = other_ref[...]
    width = c_ref.shape[1]
    factor = b_block[...].reshape(t_hbm.shape[2], width)
    gram = contract_rows(factor, factor)
    parts, rows, _ = out_ref.shape
    share = width // parts
    out_ref[:, rows - share :, :] = gram.reshape(parts, share, width)
    turned = factor.T
    c_turned = c_ref[...].T
    for k in range(slices):
        w_high, w_low = split(turned * c_turned[:, k : k + 1])
        w_both = jnp.concatenate([w_high, w_low], axis=0)
        pltpu.make_async_copy(t_hbm.at[k], t_buf.at[k], sems.at[k]).wait()
        t_high, t_low = split(t_buf[k])
        main = dot_turned(w_both, t_high)
        rest = dot_turned(w_high, t_low)
        term = main[:width] + (main[width:] + rest)
        if k == 0:
            total[...] = term
        else:
            total[...] += term
    out_ref[:, : rows - share, :] = total[...].T.reshape(parts, rows - share, width)


def sum_kernel(in_ref, out_ref):
    parts = in_ref.shape[0]
    total = in_ref[0]
    for d in range(1, parts):
        total += in_ref[d]
    out_ref[...] = jnp.broadcast_to(total[None], out_ref.shape)


def middle_kernel(own_ref, g_ref, c_ref, a_ref, scaled_ref, message_ref, block):
    parts, rows, width = g_ref.shape
    share = width // parts
    owned = rows - share
    factor_c = c_ref[...]
    system = contract_rows(factor_c, factor_c) * g_ref[:, owned:, :].reshape(width, width)
    solved = inverse(system)
    update = dot32(g_ref[:, :owned, :].reshape(parts * owned, width), solved)
    block[...] = update
    start = pl.multiple_of(own_ref[1] * owned, owned)
    a_ref[...] = block[pl.ds(start, owned), :]
    most = jnp.max(jnp.abs(update), axis=0, keepdims=True)
    most = jnp.where(most > 0.0, most, TINY)
    scaled = update * (1.0 / most)
    scaled_ref[...] = scaled
    message_ref[:width, :] = contract_rows(update, scaled)
    message_ref[width:, :] = jnp.broadcast_to(most, (message_ref.shape[0] - width, width))


def merge(mine_ref, got_ref):
    width = mine_ref.shape[1]
    mine = mine_ref[width : width + 1, :]
    got = got_ref[width : width + 1, :]
    most = jnp.maximum(mine, got)
    return mine_ref[:width, :] * (mine / most) + got_ref[:width, :] * (got / most), most


def merge_kernel(mine_ref, got_ref, out_ref):
    gram, most = merge(mine_ref, got_ref)
    width = gram.shape[1]
    out_ref[:width, :] = gram
    out_ref[width:, :] = jnp.broadcast_to(most, (out_ref.shape[0] - width, width))


def second_kernel(own_ref, t_hbm, scaled_ref, c_ref, message_ref, pair_ref, send_ref, keep_ref, total, halves, t_buf, sems):
    slices = t_hbm.shape[0]
    for k in range(slices):
        pltpu.make_async_copy(t_hbm.at[k], t_buf.at[k], sems.at[k]).start()
    turned = scaled_ref[...].T
    width = turned.shape[0]
    c_turned = c_ref[...].T
    for k in range(slices):
        w_high, w_low = split(turned * c_turned[:, k : k + 1])
        w_both = jnp.concatenate([w_high, w_low], axis=0)
        pltpu.make_async_copy(t_hbm.at[k], t_buf.at[k], sems.at[k]).wait()
        t_high, t_low = split(t_buf[k])
        main = jnp.dot(w_both, t_high, preferred_element_type=jnp.float32)
        rest = jnp.dot(w_high, t_low, preferred_element_type=jnp.float32)
        term = main[:width] + (main[width:] + rest)
        if k == 0:
            total[...] = term
        else:
            total[...] += term
    scale = message_ref[width : width + 1, :] / pair_ref[width : width + 1, :]
    halves[...] = (total[...].T * scale).reshape(halves.shape)
    core = own_ref[0]
    send_ref[...] = halves[:, 1 - core].reshape(send_ref.shape)
    keep_ref[...] = halves[:, core]


def pair_kernel(keep_ref, got_ref, pair_ref, out_ref):
    targets, owned, width = keep_ref.shape
    out_ref[:, :owned, :] = keep_ref[...] + got_ref[...].reshape(keep_ref.shape)
    out_ref[:, owned:, :] = jnp.broadcast_to(
        pair_ref[width : width + 1, :].reshape(1, 1, width),
        (targets, out_ref.shape[1] - owned, width),
    )


def solve_kernel(mine_ref, got_ref, c_ref, out_ref):
    gram, most = merge(mine_ref, got_ref)
    width = gram.shape[1]
    same = lax.broadcasted_iota(jnp.int32, (width, width), 0) == lax.broadcasted_iota(
        jnp.int32, (width, width), 1
    )
    norms = jnp.sqrt(jnp.sum(jnp.where(same, gram, 0.0), axis=0, keepdims=True) * most + EPSILON)
    flipped = jnp.sum(jnp.where(same, jnp.broadcast_to(norms, (width, width)), 0.0), axis=1, keepdims=True)
    factor_c = c_ref[...]
    system = contract_rows(factor_c, factor_c) * ((gram * (most / norms)) / flipped)
    out_ref[:width, :] = inverse(system)
    out_ref[width:, :] = jnp.broadcast_to(norms, (out_ref.shape[0] - width, width))


def last_kernel(parts_ref, solved_ref, out_ref):
    senders, _, width = parts_ref.shape
    owned = out_ref.shape[0]
    norms = solved_ref[width : width + 1, :]
    total = jnp.zeros((owned, width), jnp.float32)
    for d in range(senders):
        total += parts_ref[d, :owned, :] * (parts_ref[d, owned : owned + 1, :] / norms)
    out_ref[...] = dot32(total, solved_ref[:width, :])


def limited(mebibytes):
    return pltpu.CompilerParams(vmem_limit_bytes=mebibytes * 1024 * 1024)


def per_device(tensor, factor_b, factor_c):
    slices, rows_block, cols_block = tensor.shape
    width = factor_c.shape[1]
    row_size = lax.axis_size(ROW)
    col_size = lax.axis_size(COL)
    z_size = lax.axis_size("z")
    owned_a = rows_block // col_size
    owned_b = cols_block // row_size
    share_a = width // col_size
    f32 = jnp.float32
    shape = jax.ShapeDtypeStruct

    small = limited(WORK_MIB)
    swap = [(0, 1), (1, 0)]
    own = jnp.stack([lax.axis_index("core"), lax.axis_index(COL)]).astype(jnp.int32)
    spread_b = jnp.broadcast_to(factor_b[None], (z_size,) + factor_b.shape)
    mine = lax.all_to_all(spread_b, "z", 0, 0, tiled=True)
    other = lax.ppermute(mine, "core", swap)
    staged_c = pl.pallas_call(
        stage_kernel,
        out_shape=pltpu.VMEM(factor_c.shape, f32),
        in_specs=[VMEM],
        out_specs=VMEM,
        compiler_params=small,
        name="stage",
    )(factor_c)
    packed = pl.pallas_call(
        first_kernel,
        out_shape=shape((col_size, owned_a + share_a, width), f32),
        in_specs=[SMEM, HBM, VMEM, VMEM, VMEM],
        out_specs=VMEM,
        scratch_shapes=[
            pltpu.VMEM(tensor.shape, f32),
            pltpu.VMEM((z_size, 2, owned_b, width), f32),
            pltpu.VMEM((width, rows_block), f32),
            pltpu.SemaphoreType.DMA((slices,)),
        ],
        compiler_params=limited(LARGE_MIB),
        name="first",
    )(own, tensor, mine, other, staged_c)
    received = lax.all_to_all(packed, COL, 0, 0, tiled=True)
    summed = pl.pallas_call(
        sum_kernel,
        out_shape=shape(received.shape, f32),
        in_specs=[VMEM],
        out_specs=VMEM,
        compiler_params=limited(WORK_MIB),
        name="sum",
    )(received)
    gathered = lax.all_to_all(summed, COL, 0, 0, tiled=True)
    a_update, scaled, message = pl.pallas_call(
        middle_kernel,
        out_shape=(
            shape((owned_a, width), f32),
            shape((rows_block, width), f32),
            shape((width + 8, width), f32),
        ),
        in_specs=[SMEM, VMEM, VMEM],
        out_specs=(VMEM, VMEM, VMEM),
        scratch_shapes=[pltpu.VMEM((rows_block, width), f32)],
        compiler_params=limited(WORK_MIB),
        name="middle",
    )(own, gathered, staged_c)

    def merged(mine, got):
        return pl.pallas_call(
            merge_kernel,
            out_shape=shape(message.shape, f32),
            in_specs=[VMEM, VMEM],
            out_specs=VMEM,
            compiler_params=small,
            name="merge",
        )(mine, got)

    def flipped(array, distance):
        return lax.ppermute(array, "z", [(i, i ^ distance) for i in range(z_size)])

    got = lax.ppermute(message, "core", swap)
    pair = merged(message, got)
    got = flipped(pair, 4)
    send, keep = pl.pallas_call(
        second_kernel,
        out_shape=(
            shape((z_size * owned_b, width), f32),
            shape((z_size, owned_b, width), f32),
        ),
        in_specs=[SMEM, HBM] + [VMEM] * 4,
        out_specs=(VMEM, VMEM),
        scratch_shapes=[
            pltpu.VMEM((width, cols_block), f32),
            pltpu.VMEM((z_size, 2, owned_b, width), f32),
            pltpu.VMEM(tensor.shape, f32),
            pltpu.SemaphoreType.DMA((slices,)),
        ],
        compiler_params=limited(LARGE_MIB),
        cost_estimate=pl.CostEstimate(
            flops=6 * tensor.size * width, bytes_accessed=4 * tensor.size, transcendentals=0
        ),
        name="second",
    )(own, tensor, scaled, staged_c, message, pair)
    quad = merged(pair, got)
    other_half = lax.ppermute(send, "core", swap)
    got = flipped(quad, 1)
    octet = merged(quad, got)
    got = flipped(octet, 2)
    outgoing = pl.pallas_call(
        pair_kernel,
        out_shape=shape((z_size, owned_b + 8, width), f32),
        in_specs=[VMEM] * 3,
        out_specs=VMEM,
        compiler_params=small,
        name="pair",
    )(keep, other_half, pair)
    final = lax.all_to_all(outgoing, "z", 0, 0, tiled=True)
    solved = pl.pallas_call(
        solve_kernel,
        out_shape=shape(message.shape, f32),
        in_specs=[VMEM] * 3,
        out_specs=VMEM,
        compiler_params=small,
        cost_estimate=pl.CostEstimate(flops=10**9, bytes_accessed=10**6, transcendentals=0),
        name="solve",
    )(octet, got, staged_c)
    b_update = pl.pallas_call(
        last_kernel,
        out_shape=shape((owned_b, width), f32),
        in_specs=[VMEM, VMEM],
        out_specs=VMEM,
        compiler_params=small,
        name="last",
    )(final, solved)
    return (a_update, b_update)


def solution(mesh):
    finer = Mesh(mesh.devices.reshape(8, 2, 4, 4), ("z", "core", "x", "y"))
    placed = (P(None, ROW, COL), P(COL + ROW, None), P())

    return jax.shard_map(
        per_device,
        mesh=finer,
        in_specs=placed,
        out_specs=(P(ROW + COL, None), P(COL + ROW, None)),
        check_vma=False,
    )
```

```python
import jax
import jax.numpy as jnp
from jax import lax
from jax.experimental import pallas as pl
from jax.experimental.pallas import tpu as pltpu
from jax.sharding import Mesh
from jax.sharding import PartitionSpec as P


EPSILON = 1e-06
HIGHEST = lax.Precision.HIGHEST
VMEM = pl.BlockSpec(memory_space=pltpu.VMEM)
HBM = pl.BlockSpec(memory_space=pltpu.HBM)
SMEM = pl.BlockSpec(memory_space=pltpu.SMEM)
ROW = ("z", "core")
COL = ("x", "y")
TINY = 1e-30
READY = 7
LARGE_MIB = 52
SPLIT_MIB = 60
WORK_MIB = 12


def split(value):
    high = value.astype(jnp.bfloat16)
    low = (value - high.astype(jnp.float32)).astype(jnp.bfloat16)
    return high, low


def contract_rows(left, right):
    return lax.dot_general(
        left, right, (((0,), (0,)), ((), ())), precision=HIGHEST,
        preferred_element_type=jnp.float32,
    )


def dot32(left, right):
    return lax.dot_general(
        left, right, (((1,), (0,)), ((), ())), precision=HIGHEST,
        preferred_element_type=jnp.float32,
    )


def dot_turned(left, right):
    return lax.dot_general(
        left, right, (((1,), (1,)), ((), ())), preferred_element_type=jnp.float32
    )


def inverse(system):
    size = system.shape[0]
    lane = lax.broadcasted_iota(jnp.int32, (8, size), 1)
    sublane = lax.broadcasted_iota(jnp.int32, (8, size), 0)

    def spread(value):
        return jnp.broadcast_to(value, (8, size))

    strips = [system[8 * i : 8 * i + 8, :] for i in range(size // 8)]
    for c in range(size // 8):
        first = 8 * c
        columns = [spread(strips[c][:, first + j : first + j + 1]) for j in range(8)]
        entry = {(i, j): spread(columns[j][i : i + 1, :]) for j in range(8) for i in range(j + 1)}

        def key(i, j):
            return (i, j) if i <= j else (j, i)

        for k in range(8):
            pivot = 1.0 / entry[k, k]
            old = [entry[key(i, k)] for i in range(8)]
            part = [value * pivot for value in old]
            for i in range(8):
                for j in range(i, 8):
                    if i != k and j != k:
                        entry[i, j] = entry[i, j] - part[i] * old[j]
            for i in range(8):
                entry[key(i, k)] = -pivot if i == k else part[i]
        inside = (lane >= first) & (lane < first + 8)
        rows = [
            jnp.where(
                inside,
                jnp.where(lane == first + j, 1.0, 0.0),
                spread(strips[c][j : j + 1, :]),
            )
            for j in range(8)
        ]
        minus = []
        for i in range(8):
            terms = [entry[key(i, j)] * rows[j] for j in range(8)]
            minus.append(
                ((terms[0] + terms[1]) + (terms[2] + terms[3]))
                + ((terms[4] + terms[5]) + (terms[6] + terms[7]))
            )
        for m in range(size // 8):
            if m == c:
                continue
            terms = [
                spread(strips[m][:, first + j : first + j + 1]) * minus[j] for j in range(8)
            ]
            strips[m] = jnp.where(inside, 0.0, strips[m]) + (
                ((terms[0] + terms[1]) + (terms[2] + terms[3]))
                + ((terms[4] + terms[5]) + (terms[6] + terms[7]))
            )
        solved = minus[0]
        for i in range(1, 8):
            solved = jnp.where(sublane == i, minus[i], solved)
        strips[c] = -solved
    return jnp.concatenate(strips, axis=0)


def split_kernel(t_ref, high_ref, low_ref):
    high, low = split(t_ref[...])
    high_ref[...] = high
    low_ref[...] = low


def fetch(t_hbm, high_hbm, low_hbm, t_buf, high_buf, low_buf, sems):
    ready = high_hbm.shape[0]
    slices = t_hbm.shape[0]
    copies = []
    for k in range(slices):
        if k < ready:
            pair = (
                pltpu.make_async_copy(high_hbm.at[k], high_buf.at[k], sems.at[0, k]),
                pltpu.make_async_copy(low_hbm.at[k], low_buf.at[k], sems.at[1, k]),
            )
        else:
            pair = (pltpu.make_async_copy(t_hbm.at[k], t_buf.at[k - ready], sems.at[0, k]),)
        for copy in pair:
            copy.start()
        copies.append(pair)

    def halves(k):
        for copy in copies[k]:
            copy.wait()
        if k < ready:
            return high_buf[k], low_buf[k]
        return split(t_buf[k - ready])

    return halves


def stage_kernel(in_ref, out_ref):
    out_ref[...] = in_ref[...]


def first_kernel(own_ref, t_hbm, high_hbm, low_hbm, mine_ref, other_ref, c_ref, out_ref, b_block, total, t_buf, high_buf, low_buf, sems):
    slices = t_hbm.shape[0]
    halves_of = fetch(t_hbm, high_hbm, low_hbm, t_buf, high_buf, low_buf, sems)
    core = own_ref[0]
    b_block[:, core] = mine_ref[...]
    b_block[:, 1 - core] = other_ref[...]
    width = c_ref.shape[1]
    factor = b_block[...].reshape(t_hbm.shape[2], width)
    gram = contract_rows(factor, factor)
    parts, rows, _ = out_ref.shape
    share = width // parts
    out_ref[:, rows - share :, :] = gram.reshape(parts, share, width)
    turned = factor.T
    c_turned = c_ref[...].T
    for k in range(slices):
        w_high, w_low = split(turned * c_turned[:, k : k + 1])
        w_both = jnp.concatenate([w_high, w_low], axis=0)
        t_high, t_low = halves_of(k)
        main = dot_turned(w_both, t_high)
        rest = dot_turned(w_high, t_low)
        term = main[:width] + (main[width:] + rest)
        if k == 0:
            total[...] = term
        else:
            total[...] += term
    out_ref[:, : rows - share, :] = total[...].T.reshape(parts, rows - share, width)


def sum_kernel(in_ref, out_ref):
    parts = in_ref.shape[0]
    total = in_ref[0]
    for d in range(1, parts):
        total += in_ref[d]
    out_ref[...] = jnp.broadcast_to(total[None], out_ref.shape)


def middle_kernel(own_ref, g_ref, c_ref, a_ref, scaled_ref, message_ref, block):
    parts, rows, width = g_ref.shape
    share = width // parts
    owned = rows - share
    factor_c = c_ref[...]
    system = contract_rows(factor_c, factor_c) * g_ref[:, owned:, :].reshape(width, width)
    solved = inverse(system)
    update = dot32(g_ref[:, :owned, :].reshape(parts * owned, width), solved)
    block[...] = update
    start = pl.multiple_of(own_ref[1] * owned, owned)
    a_ref[...] = block[pl.ds(start, owned), :]
    most = jnp.max(jnp.abs(update), axis=0, keepdims=True)
    most = jnp.where(most > 0.0, most, TINY)
    scaled = update * (1.0 / most)
    scaled_ref[...] = scaled
    message_ref[:width, :] = contract_rows(update, scaled)
    message_ref[width:, :] = jnp.broadcast_to(most, (message_ref.shape[0] - width, width))


def merge(mine_ref, got_ref):
    width = mine_ref.shape[1]
    mine = mine_ref[width : width + 1, :]
    got = got_ref[width : width + 1, :]
    most = jnp.maximum(mine, got)
    return mine_ref[:width, :] * (mine / most) + got_ref[:width, :] * (got / most), most


def merge_kernel(mine_ref, got_ref, out_ref):
    gram, most = merge(mine_ref, got_ref)
    width = gram.shape[1]
    out_ref[:width, :] = gram
    out_ref[width:, :] = jnp.broadcast_to(most, (out_ref.shape[0] - width, width))


def second_kernel(own_ref, t_hbm, high_hbm, low_hbm, scaled_ref, c_ref, message_ref, pair_ref, send_ref, keep_ref, total, halves, t_buf, high_buf, low_buf, sems):
    slices = t_hbm.shape[0]
    halves_of = fetch(t_hbm, high_hbm, low_hbm, t_buf, high_buf, low_buf, sems)
    turned = scaled_ref[...].T
    width = turned.shape[0]
    c_turned = c_ref[...].T
    for k in range(slices):
        w_high, w_low = split(turned * c_turned[:, k : k + 1])
        w_both = jnp.concatenate([w_high, w_low], axis=0)
        t_high, t_low = halves_of(k)
        main = jnp.dot(w_both, t_high, preferred_element_type=jnp.float32)
        rest = jnp.dot(w_high, t_low, preferred_element_type=jnp.float32)
        term = main[:width] + (main[width:] + rest)
        if k == 0:
            total[...] = term
        else:
            total[...] += term
    scale = message_ref[width : width + 1, :] / pair_ref[width : width + 1, :]
    halves[...] = (total[...].T * scale).reshape(halves.shape)
    core = own_ref[0]
    send_ref[...] = halves[:, 1 - core].reshape(send_ref.shape)
    keep_ref[...] = halves[:, core]


def pair_kernel(keep_ref, got_ref, pair_ref, out_ref):
    targets, owned, width = keep_ref.shape
    out_ref[:, :owned, :] = keep_ref[...] + got_ref[...].reshape(keep_ref.shape)
    out_ref[:, owned:, :] = jnp.broadcast_to(
        pair_ref[width : width + 1, :].reshape(1, 1, width),
        (targets, out_ref.shape[1] - owned, width),
    )


def solve_kernel(mine_ref, got_ref, c_ref, out_ref):
    gram, most = merge(mine_ref, got_ref)
    width = gram.shape[1]
    same = lax.broadcasted_iota(jnp.int32, (width, width), 0) == lax.broadcasted_iota(
        jnp.int32, (width, width), 1
    )
    norms = jnp.sqrt(jnp.sum(jnp.where(same, gram, 0.0), axis=0, keepdims=True) * most + EPSILON)
    flipped = jnp.sum(jnp.where(same, jnp.broadcast_to(norms, (width, width)), 0.0), axis=1, keepdims=True)
    factor_c = c_ref[...]
    system = contract_rows(factor_c, factor_c) * ((gram * (most / norms)) / flipped)
    out_ref[:width, :] = inverse(system)
    out_ref[width:, :] = jnp.broadcast_to(norms, (out_ref.shape[0] - width, width))


def last_kernel(parts_ref, solved_ref, out_ref):
    senders, _, width = parts_ref.shape
    owned = out_ref.shape[0]
    norms = solved_ref[width : width + 1, :]
    total = jnp.zeros((owned, width), jnp.float32)
    for d in range(senders):
        total += parts_ref[d, :owned, :] * (parts_ref[d, owned : owned + 1, :] / norms)
    out_ref[...] = dot32(total, solved_ref[:width, :])


def limited(mebibytes):
    return pltpu.CompilerParams(vmem_limit_bytes=mebibytes * 1024 * 1024)


def per_device(tensor, factor_b, factor_c):
    slices, rows_block, cols_block = tensor.shape
    width = factor_c.shape[1]
    row_size = lax.axis_size(ROW)
    col_size = lax.axis_size(COL)
    z_size = lax.axis_size("z")
    owned_a = rows_block // col_size
    owned_b = cols_block // row_size
    share_a = width // col_size
    f32 = jnp.float32
    shape = jax.ShapeDtypeStruct

    small = limited(WORK_MIB)
    swap = [(0, 1), (1, 0)]
    own = jnp.stack([lax.axis_index("core"), lax.axis_index(COL)]).astype(jnp.int32)
    spread_b = jnp.broadcast_to(factor_b[None], (z_size,) + factor_b.shape)
    mine = lax.all_to_all(spread_b, "z", 0, 0, tiled=True)
    block = (1, rows_block, cols_block)
    high, low = pl.pallas_call(
        split_kernel,
        grid=(READY,),
        out_shape=(shape((READY,) + block[1:], jnp.bfloat16),) * 2,
        in_specs=[pl.BlockSpec(block, lambda k: (k, 0, 0))],
        out_specs=(pl.BlockSpec(block, lambda k: (k, 0, 0)),) * 2,
        compiler_params=limited(SPLIT_MIB),
        cost_estimate=pl.CostEstimate(
            flops=4 * tensor.size, bytes_accessed=8 * tensor.size, transcendentals=0
        ),
        name="split",
    )(tensor)
    slice_scratch = [
        pltpu.VMEM((slices - READY,) + block[1:], f32),
        pltpu.VMEM((READY,) + block[1:], jnp.bfloat16),
        pltpu.VMEM((READY,) + block[1:], jnp.bfloat16),
        pltpu.SemaphoreType.DMA((2, slices)),
    ]
    other = lax.ppermute(mine, "core", swap)
    staged_c = pl.pallas_call(
        stage_kernel,
        out_shape=pltpu.VMEM(factor_c.shape, f32),
        in_specs=[VMEM],
        out_specs=VMEM,
        compiler_params=small,
        name="stage",
    )(factor_c)
    packed = pl.pallas_call(
        first_kernel,
        out_shape=shape((col_size, owned_a + share_a, width), f32),
        in_specs=[SMEM] + [HBM] * 3 + [VMEM] * 3,
        out_specs=VMEM,
        scratch_shapes=[
            pltpu.VMEM((z_size, 2, owned_b, width), f32),
            pltpu.VMEM((width, rows_block), f32),
        ]
        + slice_scratch,
        compiler_params=limited(LARGE_MIB),
        name="first",
    )(own, tensor, high, low, mine, other, staged_c)
    received = lax.all_to_all(packed, COL, 0, 0, tiled=True)
    summed = pl.pallas_call(
        sum_kernel,
        out_shape=shape(received.shape, f32),
        in_specs=[VMEM],
        out_specs=VMEM,
        compiler_params=limited(WORK_MIB),
        name="sum",
    )(received)
    gathered = lax.all_to_all(summed, COL, 0, 0, tiled=True)
    a_update, scaled, message = pl.pallas_call(
        middle_kernel,
        out_shape=(
            shape((owned_a, width), f32),
            shape((rows_block, width), f32),
            shape((width + 8, width), f32),
        ),
        in_specs=[SMEM, VMEM, VMEM],
        out_specs=(VMEM, VMEM, VMEM),
        scratch_shapes=[pltpu.VMEM((rows_block, width), f32)],
        compiler_params=limited(WORK_MIB),
        name="middle",
    )(own, gathered, staged_c)

    def merged(mine, got):
        return pl.pallas_call(
            merge_kernel,
            out_shape=shape(message.shape, f32),
            in_specs=[VMEM, VMEM],
            out_specs=VMEM,
            compiler_params=small,
            name="merge",
        )(mine, got)

    def flipped(array, distance):
        return lax.ppermute(array, "z", [(i, i ^ distance) for i in range(z_size)])

    got = lax.ppermute(message, "core", swap)
    pair = merged(message, got)
    got = flipped(pair, 4)
    send, keep = pl.pallas_call(
        second_kernel,
        out_shape=(
            shape((z_size * owned_b, width), f32),
            shape((z_size, owned_b, width), f32),
        ),
        in_specs=[SMEM] + [HBM] * 3 + [VMEM] * 4,
        out_specs=(VMEM, VMEM),
        scratch_shapes=[
            pltpu.VMEM((width, cols_block), f32),
            pltpu.VMEM((z_size, 2, owned_b, width), f32),
        ]
        + slice_scratch,
        compiler_params=limited(LARGE_MIB),
        cost_estimate=pl.CostEstimate(
            flops=6 * tensor.size * width, bytes_accessed=4 * tensor.size, transcendentals=0
        ),
        name="second",
    )(own, tensor, high, low, scaled, staged_c, message, pair)
    quad = merged(pair, got)
    other_half = lax.ppermute(send, "core", swap)
    got = flipped(quad, 1)
    octet = merged(quad, got)
    got = flipped(octet, 2)
    outgoing = pl.pallas_call(
        pair_kernel,
        out_shape=shape((z_size, owned_b + 8, width), f32),
        in_specs=[VMEM] * 3,
        out_specs=VMEM,
        compiler_params=small,
        name="pair",
    )(keep, other_half, pair)
    final = lax.all_to_all(outgoing, "z", 0, 0, tiled=True)
    solved = pl.pallas_call(
        solve_kernel,
        out_shape=shape(message.shape, f32),
        in_specs=[VMEM] * 3,
        out_specs=VMEM,
        compiler_params=small,
        cost_estimate=pl.CostEstimate(flops=10**9, bytes_accessed=10**6, transcendentals=0),
        name="solve",
    )(octet, got, staged_c)
    b_update = pl.pallas_call(
        last_kernel,
        out_shape=shape((owned_b, width), f32),
        in_specs=[VMEM, VMEM],
        out_specs=VMEM,
        compiler_params=small,
        name="last",
    )(final, solved)
    return (a_update, b_update)


def solution(mesh):
    finer = Mesh(mesh.devices.reshape(8, 2, 4, 4), ("z", "core", "x", "y"))
    placed = (P(None, ROW, COL), P(COL + ROW, None), P())

    return jax.shard_map(
        per_device,
        mesh=finer,
        in_specs=placed,
        out_specs=(P(ROW + COL, None), P(COL + ROW, None)),
        check_vma=False,
    )
```

```python
import jax
import jax.numpy as jnp
from jax import lax
from jax.experimental import pallas as pl
from jax.experimental.pallas import tpu as pltpu
from jax.sharding import Mesh
from jax.sharding import PartitionSpec as P


EPSILON = 1e-06
HIGHEST = lax.Precision.HIGHEST
VMEM = pl.BlockSpec(memory_space=pltpu.VMEM)
HBM = pl.BlockSpec(memory_space=pltpu.HBM)
SMEM = pl.BlockSpec(memory_space=pltpu.SMEM)
ROW = ("z", "core")
COL = ("x", "y")
TINY = 1e-30
EARLY = 3
LARGE_MIB = 52
FIRST_MIB = 46
WORK_MIB = 12


def split(value):
    high = value.astype(jnp.bfloat16)
    low = (value - high.astype(jnp.float32)).astype(jnp.bfloat16)
    return high, low


def contract_rows(left, right):
    return lax.dot_general(
        left, right, (((0,), (0,)), ((), ())), precision=HIGHEST,
        preferred_element_type=jnp.float32,
    )


def dot32(left, right):
    return lax.dot_general(
        left, right, (((1,), (0,)), ((), ())), precision=HIGHEST,
        preferred_element_type=jnp.float32,
    )


def dot_turned(left, right):
    return lax.dot_general(
        left, right, (((1,), (1,)), ((), ())), preferred_element_type=jnp.float32
    )


def inverse(system):
    size = system.shape[0]
    lane = lax.broadcasted_iota(jnp.int32, (8, size), 1)
    sublane = lax.broadcasted_iota(jnp.int32, (8, size), 0)

    def spread(value):
        return jnp.broadcast_to(value, (8, size))

    strips = [system[8 * i : 8 * i + 8, :] for i in range(size // 8)]
    for c in range(size // 8):
        first = 8 * c
        columns = [spread(strips[c][:, first + j : first + j + 1]) for j in range(8)]
        entry = {(i, j): spread(columns[j][i : i + 1, :]) for j in range(8) for i in range(j + 1)}

        def key(i, j):
            return (i, j) if i <= j else (j, i)

        for k in range(8):
            pivot = 1.0 / entry[k, k]
            old = [entry[key(i, k)] for i in range(8)]
            part = [value * pivot for value in old]
            for i in range(8):
                for j in range(i, 8):
                    if i != k and j != k:
                        entry[i, j] = entry[i, j] - part[i] * old[j]
            for i in range(8):
                entry[key(i, k)] = -pivot if i == k else part[i]
        inside = (lane >= first) & (lane < first + 8)
        rows = [
            jnp.where(
                inside,
                jnp.where(lane == first + j, 1.0, 0.0),
                spread(strips[c][j : j + 1, :]),
            )
            for j in range(8)
        ]
        minus = []
        for i in range(8):
            terms = [entry[key(i, j)] * rows[j] for j in range(8)]
            minus.append(
                ((terms[0] + terms[1]) + (terms[2] + terms[3]))
                + ((terms[4] + terms[5]) + (terms[6] + terms[7]))
            )
        for m in range(size // 8):
            if m == c:
                continue
            terms = [
                spread(strips[m][:, first + j : first + j + 1]) * minus[j] for j in range(8)
            ]
            strips[m] = jnp.where(inside, 0.0, strips[m]) + (
                ((terms[0] + terms[1]) + (terms[2] + terms[3]))
                + ((terms[4] + terms[5]) + (terms[6] + terms[7]))
            )
        solved = minus[0]
        for i in range(1, 8):
            solved = jnp.where(sublane == i, minus[i], solved)
        strips[c] = -solved
    return jnp.concatenate(strips, axis=0)


def stage_kernel(t_hbm, out_ref, sems):
    copies = [
        pltpu.make_async_copy(t_hbm.at[k], out_ref.at[k], sems.at[k])
        for k in range(out_ref.shape[0])
    ]
    for copy in copies:
        copy.start()
    for copy in copies:
        copy.wait()


def first_kernel(own_ref, t_hbm, early_ref, mine_ref, other_ref, c_ref, out_ref, t_buf, b_block, total, sems):
    slices = t_hbm.shape[0]
    early = early_ref.shape[0]
    for k in range(early, slices):
        pltpu.make_async_copy(t_hbm.at[k], t_buf.at[k - early], sems.at[k - early]).start()
    core = own_ref[0]
    b_block[:, core] = mine_ref[...]
    b_block[:, 1 - core] = other_ref[...]
    width = c_ref.shape[1]
    factor = b_block[...].reshape(t_hbm.shape[2], width)
    gram = contract_rows(factor, factor)
    parts, rows, _ = out_ref.shape
    share = width // parts
    out_ref[:, rows - share :, :] = gram.reshape(parts, share, width)
    turned = factor.T
    c_turned = c_ref[...].T
    for k in range(slices):
        w_high, w_low = split(turned * c_turned[:, k : k + 1])
        w_both = jnp.concatenate([w_high, w_low], axis=0)
        if k < early:
            t_high, t_low = split(early_ref[k])
        else:
            pltpu.make_async_copy(t_hbm.at[k], t_buf.at[k - early], sems.at[k - early]).wait()
            t_high, t_low = split(t_buf[k - early])
        main = dot_turned(w_both, t_high)
        rest = dot_turned(w_high, t_low)
        term = main[:width] + (main[width:] + rest)
        if k == 0:
            total[...] = term
        else:
            total[...] += term
    out_ref[:, : rows - share, :] = total[...].T.reshape(parts, rows - share, width)


def sum_kernel(in_ref, out_ref):
    parts = in_ref.shape[0]
    total = in_ref[0]
    for d in range(1, parts):
        total += in_ref[d]
    out_ref[...] = jnp.broadcast_to(total[None], out_ref.shape)


def middle_kernel(own_ref, g_ref, c_ref, a_ref, scaled_ref, message_ref, block):
    parts, rows, width = g_ref.shape
    share = width // parts
    owned = rows - share
    factor_c = c_ref[...]
    system = contract_rows(factor_c, factor_c) * g_ref[:, owned:, :].reshape(width, width)
    solved = inverse(system)
    update = dot32(g_ref[:, :owned, :].reshape(parts * owned, width), solved)
    block[...] = update
    start = pl.multiple_of(own_ref[1] * owned, owned)
    a_ref[...] = block[pl.ds(start, owned), :]
    most = jnp.max(jnp.abs(update), axis=0, keepdims=True)
    most = jnp.where(most > 0.0, most, TINY)
    scaled = update * (1.0 / most)
    scaled_ref[...] = scaled
    message_ref[:width, :] = contract_rows(update, scaled)
    message_ref[width:, :] = jnp.broadcast_to(most, (message_ref.shape[0] - width, width))


def merge(mine_ref, got_ref):
    width = mine_ref.shape[1]
    mine = mine_ref[width : width + 1, :]
    got = got_ref[width : width + 1, :]
    most = jnp.maximum(mine, got)
    return mine_ref[:width, :] * (mine / most) + got_ref[:width, :] * (got / most), most


def merge_kernel(mine_ref, got_ref, out_ref):
    gram, most = merge(mine_ref, got_ref)
    width = gram.shape[1]
    out_ref[:width, :] = gram
    out_ref[width:, :] = jnp.broadcast_to(most, (out_ref.shape[0] - width, width))


def second_kernel(own_ref, t_hbm, scaled_ref, c_ref, message_ref, pair_ref, send_ref, keep_ref, total, halves, t_buf, sems):
    slices = t_hbm.shape[0]
    for k in range(slices):
        pltpu.make_async_copy(t_hbm.at[k], t_buf.at[k], sems.at[k]).start()
    turned = scaled_ref[...].T
    width = turned.shape[0]
    c_turned = c_ref[...].T
    for k in range(slices):
        w_high, w_low = split(turned * c_turned[:, k : k + 1])
        w_both = jnp.concatenate([w_high, w_low], axis=0)
        pltpu.make_async_copy(t_hbm.at[k], t_buf.at[k], sems.at[k]).wait()
        t_high, t_low = split(t_buf[k])
        main = jnp.dot(w_both, t_high, preferred_element_type=jnp.float32)
        rest = jnp.dot(w_high, t_low, preferred_element_type=jnp.float32)
        term = main[:width] + (main[width:] + rest)
        if k == 0:
            total[...] = term
        else:
            total[...] += term
    scale = message_ref[width : width + 1, :] / pair_ref[width : width + 1, :]
    halves[...] = (total[...].T * scale).reshape(halves.shape)
    core = own_ref[0]
    send_ref[...] = halves[:, 1 - core].reshape(send_ref.shape)
    keep_ref[...] = halves[:, core]


def pair_kernel(keep_ref, got_ref, pair_ref, out_ref):
    targets, owned, width = keep_ref.shape
    out_ref[:, :owned, :] = keep_ref[...] + got_ref[...].reshape(keep_ref.shape)
    out_ref[:, owned:, :] = jnp.broadcast_to(
        pair_ref[width : width + 1, :].reshape(1, 1, width),
        (targets, out_ref.shape[1] - owned, width),
    )


def solve_kernel(mine_ref, got_ref, c_ref, out_ref):
    gram, most = merge(mine_ref, got_ref)
    width = gram.shape[1]
    same = lax.broadcasted_iota(jnp.int32, (width, width), 0) == lax.broadcasted_iota(
        jnp.int32, (width, width), 1
    )
    norms = jnp.sqrt(jnp.sum(jnp.where(same, gram, 0.0), axis=0, keepdims=True) * most + EPSILON)
    flipped = jnp.sum(jnp.where(same, jnp.broadcast_to(norms, (width, width)), 0.0), axis=1, keepdims=True)
    factor_c = c_ref[...]
    system = contract_rows(factor_c, factor_c) * ((gram * (most / norms)) / flipped)
    out_ref[:width, :] = inverse(system)
    out_ref[width:, :] = jnp.broadcast_to(norms, (out_ref.shape[0] - width, width))


def last_kernel(parts_ref, solved_ref, out_ref):
    senders, _, width = parts_ref.shape
    owned = out_ref.shape[0]
    norms = solved_ref[width : width + 1, :]
    total = jnp.zeros((owned, width), jnp.float32)
    for d in range(senders):
        total += parts_ref[d, :owned, :] * (parts_ref[d, owned : owned + 1, :] / norms)
    out_ref[...] = dot32(total, solved_ref[:width, :])


def limited(mebibytes):
    return pltpu.CompilerParams(vmem_limit_bytes=mebibytes * 1024 * 1024)


def per_device(tensor, factor_b, factor_c):
    slices, rows_block, cols_block = tensor.shape
    width = factor_c.shape[1]
    row_size = lax.axis_size(ROW)
    col_size = lax.axis_size(COL)
    z_size = lax.axis_size("z")
    owned_a = rows_block // col_size
    owned_b = cols_block // row_size
    share_a = width // col_size
    f32 = jnp.float32
    shape = jax.ShapeDtypeStruct

    small = limited(WORK_MIB)
    swap = [(0, 1), (1, 0)]
    own = jnp.stack([lax.axis_index("core"), lax.axis_index(COL)]).astype(jnp.int32)
    spread_b = jnp.broadcast_to(factor_b[None], (z_size,) + factor_b.shape)
    mine = lax.all_to_all(spread_b, "z", 0, 0, tiled=True)
    other = lax.ppermute(mine, "core", swap)
    early = pl.pallas_call(
        stage_kernel,
        out_shape=pltpu.VMEM((EARLY, rows_block, cols_block), f32),
        in_specs=[HBM],
        out_specs=VMEM,
        scratch_shapes=[pltpu.SemaphoreType.DMA((EARLY,))],
        compiler_params=limited(FIRST_MIB),
        cost_estimate=pl.CostEstimate(
            flops=0, bytes_accessed=4 * EARLY * rows_block * cols_block, transcendentals=0
        ),
        name="stage",
    )(tensor)
    packed = pl.pallas_call(
        first_kernel,
        out_shape=shape((col_size, owned_a + share_a, width), f32),
        in_specs=[SMEM, HBM] + [VMEM] * 4,
        out_specs=VMEM,
        scratch_shapes=[
            pltpu.VMEM((slices - EARLY, rows_block, cols_block), f32),
            pltpu.VMEM((z_size, 2, owned_b, width), f32),
            pltpu.VMEM((width, rows_block), f32),
            pltpu.SemaphoreType.DMA((slices - EARLY,)),
        ],
        compiler_params=limited(FIRST_MIB),
        name="first",
    )(own, tensor, early, mine, other, factor_c)
    received = lax.all_to_all(packed, COL, 0, 0, tiled=True)
    summed = pl.pallas_call(
        sum_kernel,
        out_shape=shape(received.shape, f32),
        in_specs=[VMEM],
        out_specs=VMEM,
        compiler_params=limited(WORK_MIB),
        name="sum",
    )(received)
    gathered = lax.all_to_all(summed, COL, 0, 0, tiled=True)
    a_update, scaled, message = pl.pallas_call(
        middle_kernel,
        out_shape=(
            shape((owned_a, width), f32),
            shape((rows_block, width), f32),
            shape((width + 8, width), f32),
        ),
        in_specs=[SMEM, VMEM, VMEM],
        out_specs=(VMEM, VMEM, VMEM),
        scratch_shapes=[pltpu.VMEM((rows_block, width), f32)],
        compiler_params=limited(WORK_MIB),
        name="middle",
    )(own, gathered, factor_c)

    def merged(mine, got):
        return pl.pallas_call(
            merge_kernel,
            out_shape=shape(message.shape, f32),
            in_specs=[VMEM, VMEM],
            out_specs=VMEM,
            compiler_params=small,
            name="merge",
        )(mine, got)

    def flipped(array, distance):
        return lax.ppermute(array, "z", [(i, i ^ distance) for i in range(z_size)])

    got = lax.ppermute(message, "core", swap)
    pair = merged(message, got)
    got = flipped(pair, 4)
    send, keep = pl.pallas_call(
        second_kernel,
        out_shape=(
            shape((z_size * owned_b, width), f32),
            shape((z_size, owned_b, width), f32),
        ),
        in_specs=[SMEM, HBM] + [VMEM] * 4,
        out_specs=(VMEM, VMEM),
        scratch_shapes=[
            pltpu.VMEM((width, cols_block), f32),
            pltpu.VMEM((z_size, 2, owned_b, width), f32),
            pltpu.VMEM(tensor.shape, f32),
            pltpu.SemaphoreType.DMA((slices,)),
        ],
        compiler_params=limited(LARGE_MIB),
        cost_estimate=pl.CostEstimate(
            flops=6 * tensor.size * width, bytes_accessed=4 * tensor.size, transcendentals=0
        ),
        name="second",
    )(own, tensor, scaled, factor_c, message, pair)
    quad = merged(pair, got)
    other_half = lax.ppermute(send, "core", swap)
    got = flipped(quad, 2)
    octet = merged(quad, got)
    got = flipped(octet, 1)
    outgoing = pl.pallas_call(
        pair_kernel,
        out_shape=shape((z_size, owned_b + 8, width), f32),
        in_specs=[VMEM] * 3,
        out_specs=VMEM,
        compiler_params=small,
        name="pair",
    )(keep, other_half, pair)
    final = lax.all_to_all(outgoing, "z", 0, 0, tiled=True)
    solved = pl.pallas_call(
        solve_kernel,
        out_shape=shape(message.shape, f32),
        in_specs=[VMEM] * 3,
        out_specs=VMEM,
        compiler_params=small,
        cost_estimate=pl.CostEstimate(flops=10**9, bytes_accessed=10**6, transcendentals=0),
        name="solve",
    )(octet, got, factor_c)
    b_update = pl.pallas_call(
        last_kernel,
        out_shape=shape((owned_b, width), f32),
        in_specs=[VMEM, VMEM],
        out_specs=VMEM,
        compiler_params=small,
        name="last",
    )(final, solved)
    return (a_update, b_update)


def solution(mesh):
    finer = Mesh(mesh.devices.reshape(8, 2, 4, 4), ("z", "core", "x", "y"))
    placed = (P(None, ROW, COL), P(COL + ROW, None), P())

    return jax.shard_map(
        per_device,
        mesh=finer,
        in_specs=placed,
        out_specs=(P(ROW + COL, None), P(COL + ROW, None)),
        check_vma=False,
    )
```
